512 devices in a mesh: seq: 32 (over y, x), head: 16 (over z, core).
Axes of the slice: x: 4, y: 8, z: 8, core: 2. Of those that a mesh axis runs over, the one named last changes fastest.
Arguments:
- queries: bfloat16 [8192, 8192], P('seq', 'head'), may hold values from -1.796875 to 1.796875
- key_rows: bfloat16 [8192, 8192], P('seq', 'head'), may hold values from -1.796875 to 1.796875
- value_rows: bfloat16 [8192, 8192], P('seq', 'head'), may hold values from -6 to 6
- level_table: float32 [64, 7, 64], P(None, None, 'head'), may hold values from 0.25 to 4
- level_index: int32 [8192, 7], P('seq'), may hold values from 0 to 63
- norm_gain: float32 [8192], replicated, may hold values from 0.5 to 1.5
- cotangent: bfloat16 [8192, 8192], P(('seq', 'head')), may hold values from -6 to 6
Outputs:
- normed: bfloat16 [8192, 8192], P(('seq', 'head'))
- grad_query: bfloat16 [8192, 8192], P('seq', 'head')
- grad_key: bfloat16 [8192, 8192], P('seq', 'head')
- grad_value: bfloat16 [8192, 8192], P('seq', 'head')
- grad_table: float32 [64, 7, 64], P(None, None, 'head')
- grad_gain: float32 [8192], replicated
The draws below stay inside these ranges and needn't reach their ends.
All inputs are finite; a program needn't handle non-finite values.
Results may differ from the reference program's by a relative error of at most 0.014.
Values may be sent and summed in bfloat16 or wider, within the bound.
A program may use at most 64 MiB of HBM per device.

```python
import math
import jax
import jax.numpy as jnp
from jax import lax

HEADS = 64
DH = 128
CH = 128
LEVELS = 7
TABLE = 64
TOKENS = 8192


def set_ends(entries, stream_key, low, largest):
    longest = entries.shape.index(max(entries.shape))
    spots = []
    for shift in (0, 1):
        where = [jax.random.randint(jax.random.fold_in(stream_key, axis), (), 0, length) for axis, length in enumerate(entries.shape)]
        where[longest] = (where[longest] + shift) % entries.shape[longest]
        spots.append(tuple(where))
    return entries.at[spots[0]].set(low).at[spots[1]].set(largest)


def shard_levels(rng, extent, pieces, least, largest):
    def one(dim, parts):
        steps = jax.random.uniform(jax.random.fold_in(jax.random.fold_in(rng, 6), dim), (parts,), jnp.float32, least / len(pieces), largest / len(pieces))
        return jnp.repeat(jnp.exp(steps), extent[dim] // parts).reshape((-1,) + (1,) * (len(extent) - dim - 1))

    factor_of = one(*pieces[0])
    for cut in pieces[1:]:
        factor_of = factor_of * one(*cut)
    return factor_of


def gaussian(stream_key, extent, deviation, most, split=(), kind=jnp.bfloat16):
    array = jax.random.normal(stream_key, extent, jnp.float32) * deviation
    if len(split) > 0:
        array = shard_levels(stream_key, extent, split, -0.22, 0.18) * array
    return jnp.clip(array, min=-most, max=most).astype(kind)


def setup_inputs(seed: int = 0) -> dict:
    splits = jax.random.split(jax.random.key(seed), 8)
    queries = gaussian(splits[0], (TOKENS, HEADS * DH), 0.3, 1.796875, ((0, 32), (1, 16)))
    key_rows = gaussian(splits[1], (TOKENS, HEADS * DH), 0.3, 1.796875, ((0, 32), (1, 16)))
    value_rows = gaussian(splits[2], (TOKENS, HEADS * DH), 1.0, 6.0, ((0, 32), (1, 16)))
    level_table = jnp.clip(jnp.exp(math.log(4.0) - 2.7725887 * jax.random.uniform(splits[3], (TABLE, LEVELS, HEADS), jnp.float32) ** shard_levels(splits[3], (TABLE, LEVELS, HEADS), ((2, 16),), -0.2, 0.2)), 0.25, 4.0)
    level_index = set_ends(jax.random.randint(splits[4], (TOKENS, LEVELS), 0, TABLE), jax.random.fold_in(splits[4], 1), 0, TABLE - 1).astype(jnp.int32)
    norm_gain = jnp.clip(1.0 + 0.1 * jax.random.normal(splits[5], (HEADS * DH,), jnp.float32), 0.5, 1.5)
    cotangent = gaussian(splits[6], (TOKENS, HEADS * DH), 1.0, 6.0, ((0, 512),))
    return {"queries": queries, "key_rows": key_rows, "value_rows": value_rows, "level_table": level_table, "level_index": level_index, "norm_gain": norm_gain, "cotangent": cotangent}


EPSILON = 1e-06
HIGHEST = lax.Precision.HIGHEST

def rounded(values):
    return lax.optimization_barrier(values.astype(jnp.bfloat16)).astype(jnp.float32)

def causal_mask():
    row_ids = lax.broadcasted_iota(jnp.int32, (CH, CH), 0)
    col_ids = lax.broadcasted_iota(jnp.int32, (CH, CH), 1)
    return col_ids <= row_ids

def query_side(span_states):
    span_count = span_states.shape[0]
    zeros_row = jnp.zeros((1,) + span_states.shape[1:], jnp.float32)
    prefix = jnp.concatenate([zeros_row, jnp.cumsum(span_states, axis=0)], axis=0)
    span_ids = jnp.arange(span_count, dtype=jnp.int32)
    layers = []
    for level_no in range(1, LEVELS):
        if level_no < LEVELS - 1:
            block_start = jnp.left_shift(jnp.right_shift(span_ids, level_no), level_no)
            middle = jnp.minimum(block_start + (1 << level_no - 1), span_count).astype(jnp.int32)
            active = jnp.bitwise_and(jnp.right_shift(span_ids, level_no - 1), 1).astype(jnp.float32)
            layers.append((prefix[middle] - prefix[block_start]) * active[:, None, None])
        else:
            block_start = jnp.left_shift(jnp.right_shift(span_ids, level_no - 1), level_no - 1)
            layers.append(prefix[block_start])
    return jnp.stack(layers, axis=1)

def key_side(query_grads):
    span_count = query_grads.shape[0]
    span_ids = jnp.arange(span_count, dtype=jnp.int32)
    result = jnp.zeros(query_grads.shape[:1] + query_grads.shape[2:], jnp.float32)
    for level_no in range(1, LEVELS):
        part = query_grads[:, level_no - 1]
        zeros_row = jnp.zeros((1,) + part.shape[1:], jnp.float32)
        prefix = jnp.concatenate([zeros_row, jnp.cumsum(part, axis=0)], axis=0)
        if level_no < LEVELS - 1:
            aligned = jnp.left_shift(jnp.right_shift(span_ids, level_no), level_no)
            block_start = jnp.minimum(aligned + (1 << level_no - 1), span_count).astype(jnp.int32)
            block_stop = jnp.minimum(aligned + (1 << level_no), span_count).astype(jnp.int32)
            active = 1.0 - jnp.bitwise_and(jnp.right_shift(span_ids, level_no - 1), 1).astype(jnp.float32)
            result = result + (prefix[block_stop] - prefix[block_start]) * active[:, None, None]
        else:
            block_start = jnp.left_shift(jnp.right_shift(span_ids, level_no - 1) + 1, level_no - 1)
            block_start = jnp.minimum(block_start, span_count).astype(jnp.int32)
            result = result + (prefix[span_count] - prefix[block_start])
    return result

def head_forward(query_head, key_head, value_head, weight_head):
    query_f = query_head.astype(jnp.float32)
    key_f = key_head.astype(jnp.float32)
    value_f = value_head.astype(jnp.float32)
    span_states = jnp.einsum('ica,icb->iab', key_f, value_f, precision=HIGHEST)
    states = rounded(query_side(span_states))
    far_out = jnp.einsum('ica,ilab->iclb', query_f, states, precision=HIGHEST)
    scores = jnp.einsum('ica,ina->icn', query_f, key_f, precision=HIGHEST)
    scores = jnp.where(causal_mask()[None], scores, 0.0)
    near_out = jnp.einsum('icn,inb->icb', rounded(scores), value_f, precision=HIGHEST)
    level_out = jnp.concatenate([near_out[:, :, None], far_out], axis=2)
    attn = lax.optimization_barrier(jnp.sum(weight_head[..., None] * level_out, axis=2))
    return (attn.astype(jnp.bfloat16), level_out, states, scores)

def head_backward(query_head, key_head, value_head, weight_head, grad_head):
    attn, level_out, states, scores = head_forward(query_head, key_head, value_head, weight_head)
    query_f = query_head.astype(jnp.float32)
    key_f = key_head.astype(jnp.float32)
    value_f = value_head.astype(jnp.float32)
    grad_f = grad_head.astype(jnp.float32)
    causal = causal_mask()[None]
    grad_weight = lax.optimization_barrier(jnp.sum(level_out * grad_f[:, :, None], axis=3))
    along_values = jnp.einsum('icb,inb->icn', grad_f, value_f, precision=HIGHEST)
    first_weight = weight_head[:, :, 0][:, :, None]
    grad_scores = rounded(jnp.where(causal, along_values * first_weight, 0.0))
    weighted_scores = rounded(jnp.where(causal, scores * first_weight, 0.0))
    near_dq = jnp.einsum('icn,ina->ica', grad_scores, key_f, precision=HIGHEST)
    near_dk = jnp.einsum('icn,ica->ina', grad_scores, query_f, precision=HIGHEST)
    near_dv = jnp.einsum('icn,icb->inb', weighted_scores, grad_f, precision=HIGHEST)
    far_dq = jnp.einsum('icb,ilab->icla', grad_f, states, precision=HIGHEST)
    grad_query = (near_dq + lax.optimization_barrier(jnp.sum(weight_head[:, :, 1:, None] * far_dq, axis=2))).astype(jnp.bfloat16)
    scaled_grad = rounded(weight_head[:, :, 1:, None] * grad_f[:, :, None])
    query_grads = jnp.einsum('ica,iclb->ilab', query_f, scaled_grad, precision=HIGHEST)
    key_state = rounded(key_side(query_grads))
    grad_key = (near_dk + jnp.einsum('jab,jnb->jna', key_state, value_f, precision=HIGHEST)).astype(jnp.bfloat16)
    grad_value = (near_dv + jnp.einsum('jab,jna->jnb', key_state, key_f, precision=HIGHEST)).astype(jnp.bfloat16)
    return (grad_query, grad_key, grad_value, grad_weight)

def split_heads(rows):
    return rows.reshape(TOKENS, HEADS, DH).transpose(1, 0, 2).reshape(HEADS, TOKENS // CH, CH, DH)

def join_heads(blocks):
    return blocks.reshape(HEADS, TOKENS, DH).transpose(1, 0, 2).reshape(TOKENS, HEADS * DH)

def reference(queries, key_rows, value_rows, level_table, level_index, norm_gain, cotangent):
    onehot = (level_index[:, :, None] == jnp.arange(TABLE, dtype=jnp.int32)[None, None, :]).astype(jnp.float32)
    weights = jnp.einsum('tlx,xlh->htl', onehot, level_table.astype(jnp.float32), precision=HIGHEST)
    weights = weights.reshape(HEADS, TOKENS // CH, CH, LEVELS)
    query_heads = split_heads(queries)
    key_heads = split_heads(key_rows)
    value_heads = split_heads(value_rows)

    def forward_one(operands):
        return head_forward(operands[0], operands[1], operands[2], operands[3])[0]
    attn = join_heads(lax.map(forward_one, (query_heads, key_heads, value_heads, weights)))
    attn_f = attn.astype(jnp.float32)
    inv_rms = lax.rsqrt(lax.optimization_barrier(jnp.mean(attn_f * attn_f, axis=1, keepdims=True)) + EPSILON)
    unit_rows = attn_f * inv_rms
    gain_f = norm_gain.astype(jnp.float32)
    normed = (unit_rows * gain_f).astype(jnp.bfloat16)
    grad_out = cotangent.astype(jnp.float32)
    scaled = grad_out * gain_f
    grad_gain = lax.optimization_barrier(jnp.sum(grad_out * unit_rows, axis=0))
    grad_attn = ((scaled - unit_rows * lax.optimization_barrier(jnp.mean(scaled * unit_rows, axis=1, keepdims=True))) * inv_rms).astype(jnp.bfloat16)
    grad_heads = split_heads(grad_attn)

    def backward_one(operands):
        return head_backward(operands[0], operands[1], operands[2], operands[3], operands[4])
    grad_query, grad_key, grad_value, grad_weight = lax.map(backward_one, (query_heads, key_heads, value_heads, weights, grad_heads))
    grad_table = jnp.einsum('tlx,htl->xlh', onehot, grad_weight.reshape(HEADS, TOKENS, LEVELS), precision=HIGHEST)
    return (normed, join_heads(grad_query), join_heads(grad_key), join_heads(grad_value), grad_table, grad_gain)
```

```python
import functools

import jax
import jax.numpy as jnp
from jax import lax
from jax.experimental import pallas as pl
from jax.experimental.pallas import tpu as pltpu
from jax.sharding import PartitionSpec as P

CH = 128
DH = 128
EPSILON = 1e-06
MESH = pl.DeviceIdType.MESH
F32 = jnp.float32
BF16 = jnp.bfloat16

NN = (((1,), (0,)), ((), ()))
NT = (((1,), (1,)), ((), ()))
TN = (((0,), (0,)), ((), ()))


def mm(a, b, dims):
    return lax.dot_general(a, b, dims, preferred_element_type=F32)


def split_two(value):
    high = value.astype(BF16)
    low = (value - high.astype(F32)).astype(BF16)
    return high, low


def bit_of(index, place):
    return lax.rem(lax.div(index, jnp.int32(2**place)), jnp.int32(2))


def send(src, dst, send_sem, recv_sem, axis, target):
    pltpu.make_async_remote_copy(
        src_ref=src,
        dst_ref=dst,
        send_sem=send_sem,
        recv_sem=recv_sem,
        device_id={axis: target},
        device_id_type=MESH,
    ).start()


def drain(view, sem):
    pltpu.make_async_copy(view, view, sem).wait()


def kernel(
    shards,
    members,
    q_in,
    k_in,
    v_in,
    tab_in,
    idx_in,
    gain_in,
    cot_in,
    normed_out,
    dq_out,
    dk_out,
    dv_out,
    gtab_out,
    ggain_out,
    q,
    k,
    v,
    tab,
    idx,
    gain,
    cot,
    total,
    total_in,
    level,
    level_in,
    state,
    intra,
    weight,
    out,
    scores,
    attn,
    stat,
    stat_in,
    normed,
    gpart,
    gpart_in,
    gsum,
    gall,
    grad,
    qg,
    qg_in,
    inner,
    ks,
    ks_in,
    dq,
    dk,
    dv,
    dk_bf,
    dv_bf,
    tpart,
    tpart_in,
    tsum,
    load_sem,
    store_sem,
    send_sem,
    recv_sem,
    tab_sem,
):
    me = lax.axis_index("seq")
    mine = lax.axis_index("head")
    bits = shards.bit_length() - 1
    toks, width = q.shape
    heads = width // DH
    levels = bits + 2
    rows = heads * DH // shards
    group = shards // heads
    piece = toks // members
    table = tab.shape[2]
    features = members * width

    def head_cols(h):
        return slice(h * DH, (h + 1) * DH)

    def span_rows(i):
        return slice(i * CH, (i + 1) * CH)

    def seq_peers(step):
        def one(offset, carry):
            step(lax.rem(me + offset, jnp.int32(shards)))
            return carry

        lax.fori_loop(1, shards, one, 0)

    def head_peers(step):
        def one(offset, carry):
            step(lax.rem(mine + offset, jnp.int32(members)))
            return carry

        lax.fori_loop(1, members, one, 0)

    def ones_in(index):
        count = bit_of(index, 0)
        for place in range(1, bits):
            count = count + bit_of(index, place)
        return count

    my_count = ones_in(me)
    my_cols = pl.ds(pl.multiple_of(mine * width, width), width)

    loads = [
        pltpu.make_async_copy(k_in, k, load_sem.at[0]),
        pltpu.make_async_copy(v_in, v, load_sem.at[1]),
        pltpu.make_async_copy(q_in, q, load_sem.at[2]),
        pltpu.make_async_copy(tab_in, tab, load_sem.at[3]),
        pltpu.make_async_copy(idx_in, idx, load_sem.at[4]),
        pltpu.make_async_copy(gain_in.at[:, my_cols], gain, load_sem.at[5]),
        pltpu.make_async_copy(
            cot_in.at[:, my_cols],
            cot.at[pl.ds(pl.multiple_of(mine * piece, piece), piece)],
            load_sem.at[6],
        ),
    ]
    for copy in loads:
        copy.start()

    barrier = pltpu.get_barrier_semaphore()

    def greet_seq(peer):
        pl.semaphore_signal(barrier, inc=1, device_id={"seq": peer}, device_id_type=MESH)

    def greet_head(peer):
        pl.semaphore_signal(barrier, inc=1, device_id={"head": peer}, device_id_type=MESH)

    seq_peers(greet_seq)
    head_peers(greet_head)

    loads[0].wait()
    loads[1].wait()
    for h in range(heads):
        first = mm(k[span_rows(0), head_cols(h)], v[span_rows(0), head_cols(h)], TN)
        second = mm(k[span_rows(1), head_cols(h)], v[span_rows(1), head_cols(h)], TN)
        intra[h] = first.astype(BF16)
        total[h * DH : (h + 1) * DH, :] = (first + second).astype(BF16)

    pl.semaphore_wait(barrier, shards + members - 2)

    def send_total(peer):
        send(
            total.at[pl.ds(pl.multiple_of(peer * rows, rows), rows)],
            total_in.at[me],
            send_sem.at[0],
            recv_sem.at[0],
            "seq",
            peer,
        )

    seq_peers(send_total)

    def send_cot(peer):
        send(
            cot_in.at[:, pl.ds(pl.multiple_of(peer * width, width), width)],
            cot.at[pl.ds(pl.multiple_of(mine * piece, piece), piece)],
            send_sem.at[1],
            recv_sem.at[1],
            "head",
            peer,
        )

    head_peers(send_cot)
    total_in[me] = total[pl.ds(pl.multiple_of(me * rows, rows), rows), :]

    for copy in loads[2:6]:
        copy.wait()
    x_ids = lax.broadcasted_iota(jnp.int32, (table, toks), 0)
    stacked = []
    for l in range(levels):
        onehot = (idx[l : l + 1, :] == x_ids).astype(F32).astype(BF16)
        high, low = split_two(tab[l])
        stacked.append(mm(high, onehot, NN))
        stacked.append(mm(low, onehot, NN))
    pad = 128 - 2 * heads * levels
    stacked.append(jnp.zeros((pad, toks), F32))
    columns = jnp.transpose(jnp.concatenate(stacked, axis=0)).astype(BF16)
    row_ids = lax.broadcasted_iota(jnp.int32, (128, width), 0)
    col_head = lax.broadcasted_iota(jnp.int32, (128, width), 1) // DH
    for l in range(levels):
        base = 2 * heads * l
        pick = (row_ids == base + col_head) | (row_ids == base + heads + col_head)
        weight[l] = mm(columns, pick.astype(F32).astype(BF16), NN)

    causal = lax.broadcasted_iota(jnp.int32, (CH, CH), 1) <= lax.broadcasted_iota(
        jnp.int32, (CH, CH), 0
    )
    for h in range(heads):
        for i in range(2):
            at = (span_rows(i), head_cols(h))
            score = jnp.where(causal, mm(q[at], k[at], NT), 0.0)
            scores[2 * h + i] = score
            out[0, at[0], at[1]] = mm(score.astype(BF16), v[at], NN)
        out[1, span_rows(0), head_cols(h)] = jnp.zeros((CH, DH), F32)
        out[1, span_rows(1), head_cols(h)] = mm(
            q[span_rows(1), head_cols(h)], intra[h], NN
        )

    drain(total_in.at[0 : shards - 1], recv_sem.at[0])
    sums = [[total_in[c].astype(F32) for c in range(shards)]]
    for place in range(1, bits):
        below = sums[-1]
        sums.append([below[2 * j] + below[2 * j + 1] for j in range(len(below) // 2)])
    for c in range(shards):
        slot = 0
        for place in range(bits):
            if (c >> place) & 1:
                level[c * bits + slot] = sums[place][(c >> place) ^ 1].astype(BF16)
                slot += 1

    def send_level(peer):
        count = ones_in(peer)
        for n in range(1, bits + 1):

            @pl.when(count == n)
            def _():
                send(
                    level.at[pl.ds(peer * bits, n)],
                    level_in.at[pl.ds(me * bits, n)],
                    send_sem.at[2],
                    recv_sem.at[2],
                    "seq",
                    peer,
                )

    seq_peers(send_level)
    level_in[pl.ds(me * bits, bits)] = level[pl.ds(me * bits, bits)]
    for n in range(1, bits + 1):

        @pl.when(my_count == n)
        def _():
            drain(level_in.at[0 : (shards - 1) * n], recv_sem.at[2])

    slot = jnp.int32(0)
    slots = []
    for place in range(bits):
        mark = bit_of(me, place)
        slots.append(slot)
        for h in range(heads):

            @pl.when(mark == 1)
            def _():
                for g in range(group):
                    state[h, g * rows : (g + 1) * rows, place * DH : (place + 1) * DH] = level_in[
                        (h * group + g) * bits + slot
                    ]

            @pl.when(mark == 0)
            def _():
                state[h, :, place * DH : (place + 1) * DH] = jnp.zeros((DH, DH), BF16)

        slot = slot + mark

    loads[6].wait()
    drain(cot.at[0 : toks - piece], recv_sem.at[1])
    squares = jnp.zeros((toks, DH), F32)
    crosses = jnp.zeros((toks, DH), F32)
    for h in range(heads):
        cols = head_cols(h)
        far = mm(q[:, cols], state[h], NN)
        value = weight[0, :, cols] * out[0, :, cols] + weight[1, :, cols] * out[1, :, cols]
        for place in range(bits):
            part = far[:, place * DH : (place + 1) * DH]
            out[place + 2, :, cols] = part
            value = value + weight[place + 2, :, cols] * part
        value = value.astype(BF16)
        attn[:, cols] = value
        value = value.astype(F32)
        squares = squares + value * value
        crosses = crosses + cot[:, cols].astype(F32) * gain[:, cols] * value
    one_row = jnp.ones((8, DH), BF16)
    for row, part in enumerate((squares, crosses)):
        high, low = split_two(part)
        both = mm(one_row, high, NT) + mm(one_row, low, NT)
        stat[row : row + 1, :] = both[0:1, :]

    def send_stat(peer):
        send(stat, stat_in.at[mine], send_sem.at[3], recv_sem.at[3], "head", peer)

    head_peers(send_stat)
    stat_in[mine] = stat[...]
    drain(stat_in.at[0 : members - 1], recv_sem.at[3])
    both = stat_in[0]
    for m in range(1, members):
        both = both + stat_in[m]
    inv_row = lax.rsqrt(both[0:1, :] * (1.0 / features) + EPSILON)
    mean_row = both[1:2, :] * inv_row * (1.0 / features)
    inv = jnp.transpose(jnp.broadcast_to(inv_row, (DH, toks)))
    mean = jnp.transpose(jnp.broadcast_to(mean_row, (DH, toks)))

    for h in range(heads):
        cols = head_cols(h)
        unit = attn[:, cols].astype(F32) * inv
        cot_f = cot[:, cols].astype(F32)
        normed[:, cols] = (unit * gain[:, cols]).astype(BF16)
        grad[:, cols] = ((cot_f * gain[:, cols] - unit * mean) * inv).astype(BF16)
        gpart[:, cols] = jnp.sum(cot_f * unit, axis=0, keepdims=True)

    for h in range(heads):
        cols = head_cols(h)
        grad_f = grad[:, cols].astype(F32)
        scaled = [
            (weight[place + 2, :, cols] * grad_f).astype(BF16) for place in range(bits)
        ]
        products = mm(q[:, cols], jnp.concatenate(scaled, axis=1), TN)
        for place in range(bits):

            @pl.when(bit_of(me, place) == 1)
            def _():
                for g in range(group):
                    qg[(h * group + g) * bits + slots[place]] = products[
                        g * rows : (g + 1) * rows, place * DH : (place + 1) * DH
                    ].astype(BF16)

    for n in range(1, bits + 1):

        @pl.when(my_count == n)
        def _():
            def send_qg(peer):
                send(
                    qg.at[pl.ds(peer * bits, n)],
                    qg_in.at[pl.ds(me * bits, n)],
                    send_sem.at[4],
                    recv_sem.at[4],
                    "seq",
                    peer,
                )

            seq_peers(send_qg)

    qg_in[pl.ds(me * bits, bits)] = qg[pl.ds(me * bits, bits)]

    own_rows = pl.ds(pl.multiple_of(mine * piece, piece), piece)

    def send_normed(peer):
        send(
            normed.at[pl.ds(pl.multiple_of(peer * piece, piece), piece)],
            normed_out.at[:, my_cols],
            send_sem.at[5],
            recv_sem.at[5],
            "head",
            peer,
        )

    head_peers(send_normed)
    keep_normed = pltpu.make_async_copy(
        normed.at[own_rows], normed_out.at[:, my_cols], store_sem.at[0]
    )
    keep_normed.start()

    def send_gain(peer):
        send(gpart, gpart_in.at[me], send_sem.at[6], recv_sem.at[6], "seq", peer)

    seq_peers(send_gain)
    gpart_in[me] = gpart[...]

    lane_ids = lax.broadcasted_iota(jnp.int32, (8, width), 1) // DH
    head_rows = (
        (lax.broadcasted_iota(jnp.int32, (8, width), 0) == lane_ids).astype(F32).astype(BF16)
    )
    grad_all = grad[...].astype(F32)
    for l in range(levels):
        onehot = (idx[l : l + 1, :] == x_ids).astype(F32).astype(BF16)
        high, low = split_two(out[l] * grad_all)
        by_row = mm(onehot, high, NN) + mm(onehot, low, NN)
        high, low = split_two(by_row)
        result = mm(head_rows, high, NT) + mm(head_rows, low, NT)
        tpart[l] = result[0:heads, :]
    for l in range(levels):

        @pl.when(me != l)
        def _():
            send(tpart.at[l], tpart_in.at[me], send_sem.at[7], recv_sem.at[7], "seq", l)

        @pl.when(me == l)
        def _():
            tpart_in[me] = tpart[l]

    drain(gpart_in.at[0 : shards - 1], recv_sem.at[6])
    both = gpart_in[0]
    for c in range(1, shards):
        both = both + gpart_in[c]
    gsum[...] = both

    def send_gsum(peer):
        send(gsum, gall.at[:, my_cols], send_sem.at[8], recv_sem.at[8], "head", peer)

    head_peers(send_gsum)
    gall[:, my_cols] = both

    for h in range(heads):
        cols = head_cols(h)
        grad_h = grad[:, cols]
        grad_f = grad_h.astype(F32)
        scaled = [
            (weight[place + 2, :, cols] * grad_f).astype(BF16) for place in range(bits)
        ]
        far = mm(jnp.concatenate(scaled, axis=1), state[h], NT)
        near = (weight[1, span_rows(1), cols] * grad_f[CH:]).astype(BF16)
        inner[h] = mm(q[span_rows(1), cols], near, TN)
        for i in range(2):
            at = (span_rows(i), cols)
            along = mm(grad_h[span_rows(i)], v[at], NT)
            first = weight[0, span_rows(i), cols]
            grad_scores = jnp.where(causal, along * first, 0.0).astype(BF16)
            weighted = (scores[2 * h + i] * first).astype(BF16)
            value = far[span_rows(i)] + mm(grad_scores, k[at], NN)
            if i == 1:
                value = value + mm(near, intra[h], NT)
            dq[at] = value.astype(BF16)
            dk[at] = mm(grad_scores, q[at], TN)
            dv[at] = mm(weighted, grad_h[span_rows(i)], TN)
    for n in range(0, bits + 1):

        @pl.when(my_count == n)
        def _():
            drain(qg_in.at[0 : bits * shards // 2 - n], recv_sem.at[4])

    def slot_of(c, place):
        return bin(c & ((1 << place) - 1)).count("1")

    reach = [None]
    for place in range(bits - 1, -1, -1):
        reach_next = []
        for block, above in enumerate(reach):
            upper = range((2 * block + 1) << place, (2 * block + 2) << place)
            part = functools.reduce(
                lambda a, b: a + b, [qg_in[c * bits + slot_of(c, place)].astype(F32) for c in upper]
            )
            reach_next.append(part if above is None else above + part)
            reach_next.append(above)
        reach = reach_next
    for c in range(shards):
        ks[c] = jnp.zeros((rows, DH), BF16) if reach[c] is None else reach[c].astype(BF16)

    def send_ks(peer):
        send(ks.at[peer], ks_in.at[me], send_sem.at[9], recv_sem.at[9], "seq", peer)

    seq_peers(send_ks)
    ks_in[me] = ks[me]

    for l in range(levels):

        @pl.when(me == l)
        def _():
            drain(tpart_in.at[0 : shards - 1], recv_sem.at[7])
            both = tpart_in[0]
            for c in range(1, shards):
                both = both + tpart_in[c]
            tsum[l] = both

            def send_tsum(peer):
                send(tsum.at[l], tsum.at[l], send_sem.at[10], tab_sem.at[l], "seq", peer)

            seq_peers(send_tsum)

    keep_dq = pltpu.make_async_copy(dq, dq_out, store_sem.at[1])
    keep_dq.start()

    drain(ks_in.at[0 : shards - 1], recv_sem.at[9])
    for h in range(heads):
        cols = head_cols(h)
        cross = ks_in[h * group : (h + 1) * group].reshape(DH, DH)
        for i in range(2):
            at = (span_rows(i), cols)
            key_state = cross
            if i == 0:
                key_state = (cross.astype(F32) + inner[h]).astype(BF16)
            dk_bf[at] = (dk[at] + mm(v[at], key_state, NT)).astype(BF16)
            dv_bf[at] = (dv[at] + mm(k[at], key_state, NN)).astype(BF16)

    stores = [
        pltpu.make_async_copy(dk_bf, dk_out, store_sem.at[2]),
        pltpu.make_async_copy(dv_bf, dv_out, store_sem.at[3]),
    ]
    for copy in stores:
        copy.start()

    drain(gall.at[:, 0 : features - width], recv_sem.at[8])
    for l in range(levels):

        @pl.when(me != l)
        def _():
            drain(tsum.at[l], tab_sem.at[l])

    stores += [
        keep_normed,
        keep_dq,
        pltpu.make_async_copy(gall, ggain_out, store_sem.at[4]),
        pltpu.make_async_copy(tsum, gtab_out, store_sem.at[5]),
    ]
    stores[-2].start()
    stores[-1].start()
    drain(normed_out.at[:, 0 : features - width], recv_sem.at[5])
    drain(total.at[0 : (shards - 1) * rows], send_sem.at[0])
    drain(cot.at[0 : toks - piece], send_sem.at[1])
    drain(stat_in.at[0 : members - 1], send_sem.at[3])
    for n in range(0, bits + 1):

        @pl.when(my_count == n)
        def _():
            drain(level.at[0 : bits * shards // 2 - n], send_sem.at[2])
            if n:
                drain(qg.at[0 : (shards - 1) * n], send_sem.at[4])

    drain(normed.at[0 : toks - piece], send_sem.at[5])
    drain(gpart_in.at[0 : shards - 1], send_sem.at[6])
    drain(gall.at[:, 0 : features - width], send_sem.at[8])
    drain(ks_in.at[0 : shards - 1], send_sem.at[9])

    @pl.when(me < levels)
    def _():
        drain(tpart.at[0 : levels - 1], send_sem.at[7])
        drain(tpart_in.at[0 : shards - 1], send_sem.at[10])

    @pl.when(me >= levels)
    def _():
        drain(tpart, send_sem.at[7])

    for copy in stores:
        copy.wait()


def body(shards, members, queries, key_rows, value_rows, level_table, level_index, norm_gain, cotangent):
    toks, width = queries.shape
    table, levels, heads = level_table.shape
    features = norm_gain.shape[0]
    bits = shards.bit_length() - 1
    rows = heads * DH // shards
    any_space = pl.BlockSpec(memory_space=pl.ANY)
    vmem = pltpu.VMEM
    outs = pl.pallas_call(
        functools.partial(kernel, shards, members),
        out_shape=(
            jax.ShapeDtypeStruct(cotangent.shape, BF16),
            jax.ShapeDtypeStruct((toks, width), BF16),
            jax.ShapeDtypeStruct((toks, width), BF16),
            jax.ShapeDtypeStruct((toks, width), BF16),
            jax.ShapeDtypeStruct((levels, heads, table), F32),
            jax.ShapeDtypeStruct((1, features), F32),
        ),
        in_specs=[any_space] * 7,
        out_specs=[any_space] * 6,
        scratch_shapes=[
            vmem((toks, width), BF16),
            vmem((toks, width), BF16),
            vmem((toks, width), BF16),
            vmem((levels, heads, table), F32),
            vmem((levels, toks), jnp.int32),
            vmem((1, width), F32),
            vmem((toks, width), BF16),
            vmem((heads * DH, DH), BF16),
            vmem((shards, rows, DH), BF16),
            vmem((shards * bits, rows, DH), BF16),
            vmem((shards * bits, rows, DH), BF16),
            vmem((heads, DH, bits * DH), BF16),
            vmem((heads, DH, DH), BF16),
            vmem((levels, toks, width), F32),
            vmem((levels, toks, width), F32),
            vmem((2 * heads, CH, CH), F32),
            vmem((toks, width), BF16),
            vmem((2, toks), F32),
            vmem((members, 2, toks), F32),
            vmem((toks, width), BF16),
            vmem((1, width), F32),
            vmem((shards, 1, width), F32),
            vmem((1, width), F32),
            vmem((1, features), F32),
            vmem((toks, width), BF16),
            vmem((shards * bits, rows, DH), BF16),
            vmem((shards * bits, rows, DH), BF16),
            vmem((heads, DH, DH), F32),
            vmem((shards, rows, DH), BF16),
            vmem((shards, rows, DH), BF16),
            vmem((toks, width), BF16),
            vmem((toks, width), F32),
            vmem((toks, width), F32),
            vmem((toks, width), BF16),
            vmem((toks, width), BF16),
            vmem((levels, heads, table), F32),
            vmem((shards, heads, table), F32),
            vmem((levels, heads, table), F32),
            pltpu.SemaphoreType.DMA((7,)),
            pltpu.SemaphoreType.DMA((6,)),
            pltpu.SemaphoreType.DMA((11,)),
            pltpu.SemaphoreType.DMA((10,)),
            pltpu.SemaphoreType.DMA((levels,)),
        ],
        compiler_params=pltpu.CompilerParams(
            collective_id=0, has_side_effects=True, vmem_limit_bytes=48 * 2**20
        ),
    )(
        queries,
        key_rows,
        value_rows,
        jnp.transpose(level_table, (1, 2, 0)),
        jnp.transpose(level_index),
        norm_gain.reshape(1, features),
        cotangent,
    )
    normed, dq, dk, dv, gtab, ggain = outs
    return normed, dq, dk, dv, jnp.transpose(gtab, (2, 0, 1)), ggain.reshape(features)


def solution(mesh):
    wide = P("seq", "head")
    rows = P(("seq", "head"), None)
    table = P(None, None, "head")
    return jax.shard_map(
        functools.partial(body, mesh.shape["seq"], mesh.shape["head"]),
        mesh=mesh,
        in_specs=(wide, wide, wide, table, P("seq", None), P(), rows),
        out_specs=(rows, wide, wide, wide, table, P()),
        check_vma=False,
    )
```

```python
import functools

import jax
import jax.numpy as jnp
from jax import lax
from jax.experimental import pallas as pl
from jax.experimental.pallas import tpu as pltpu
from jax.sharding import PartitionSpec as P

CH = 128
DH = 128
EPSILON = 1e-06
NX = 4
VMEM_BYTES = 48 * 2**20
MESH = pl.DeviceIdType.MESH
F32 = jnp.float32
BF16 = jnp.bfloat16

NN = (((1,), (0,)), ((), ()))
NT = (((1,), (1,)), ((), ()))
TN = (((0,), (0,)), ((), ()))


def mm(a, b, dims):
    return lax.dot_general(a, b, dims, preferred_element_type=F32)


def split_two(value):
    high = value.astype(BF16)
    low = (value - high.astype(F32)).astype(BF16)
    return high, low


def bit_of(index, place):
    return lax.rem(lax.div(index, jnp.int32(2**place)), jnp.int32(2))


def send(src, dst, send_sem, recv_sem, axis, target):
    pltpu.make_async_remote_copy(
        src_ref=src,
        dst_ref=dst,
        send_sem=send_sem,
        recv_sem=recv_sem,
        device_id={axis: target},
        device_id_type=MESH,
    ).start()


def drain(view, sem):
    pltpu.make_async_copy(view, view, sem).wait()


def kernel(
    shards,
    members,
    q_in,
    k_in,
    v_in,
    tab_in,
    idx_in,
    gain_in,
    cot_in,
    normed_out,
    dq,
    dk_bf,
    dv_bf,
    tsum,
    gall,
    q,
    k,
    v,
    tab,
    idx,
    gain,
    cot,
    total,
    total_in,
    level,
    level_in,
    state,
    intra,
    weight,
    out,
    scores,
    attn,
    stat,
    stat_in,
    normed,
    gpart,
    gpart_in,
    gsum,
    grad,
    qg,
    qg_in,
    inner,
    ks,
    ks_in,
    dk,
    dv,
    tpart,
    tpart_in,
    near,
    goal,
    weighted,
    scaled,
    load_sem,
    send_sem,
    recv_sem,
    tab_sem,
):
    me = lax.axis_index("seq")
    mine = lax.axis_index("head")
    bits = shards.bit_length() - 1
    toks, width = q.shape
    heads = width // DH
    levels = bits + 2
    rows = heads * DH // shards
    group = shards // heads
    piece = toks // members
    table = tab.shape[2]
    features = members * width

    def head_cols(h):
        return slice(h * DH, (h + 1) * DH)

    def span_rows(i):
        return slice(i * CH, (i + 1) * CH)

    def from_far(index, count):
        step = lax.rem(index, jnp.int32(2))
        return count // 2 + (1 - 2 * step) * lax.div(index + 1, jnp.int32(2))

    def seq_peers(step):
        def one(index, carry):
            down = lax.div(me, jnp.int32(NX)) + from_far(lax.div(index, jnp.int32(NX)), shards // NX)
            across = lax.rem(me, jnp.int32(NX)) + from_far(lax.rem(index, jnp.int32(NX)), NX)
            step(lax.rem(down, jnp.int32(shards // NX)) * NX + lax.rem(across, jnp.int32(NX)))
            return carry

        lax.fori_loop(0, shards - 1, one, 0)

    def head_peers(step):
        def one(index, carry):
            along = lax.div(mine, jnp.int32(2)) + from_far(lax.div(index, jnp.int32(2)), members // 2)
            core = lax.rem(mine, jnp.int32(2)) + from_far(lax.rem(index, jnp.int32(2)), 2)
            step(lax.rem(along, jnp.int32(members // 2)) * 2 + lax.rem(core, jnp.int32(2)))
            return carry

        lax.fori_loop(0, members - 1, one, 0)

    def ones_in(index):
        count = bit_of(index, 0)
        for place in range(1, bits):
            count = count + bit_of(index, place)
        return count

    my_count = ones_in(me)
    my_cols = pl.ds(pl.multiple_of(mine * width, width), width)

    loads = [
        pltpu.make_async_copy(k_in, k, load_sem.at[0]),
        pltpu.make_async_copy(v_in, v, load_sem.at[1]),
        pltpu.make_async_copy(q_in, q, load_sem.at[2]),
        pltpu.make_async_copy(tab_in, tab, load_sem.at[3]),
        pltpu.make_async_copy(idx_in, idx, load_sem.at[4]),
        pltpu.make_async_copy(gain_in.at[:, my_cols], gain, load_sem.at[5]),
        pltpu.make_async_copy(
            cot_in.at[:, my_cols],
            cot.at[pl.ds(pl.multiple_of(mine * piece, piece), piece)],
            load_sem.at[6],
        ),
    ]
    for copy in loads:
        copy.start()

    barrier = pltpu.get_barrier_semaphore()

    def greet_seq(peer):
        pl.semaphore_signal(barrier, inc=1, device_id={"seq": peer}, device_id_type=MESH)

    def greet_head(peer):
        pl.semaphore_signal(barrier, inc=1, device_id={"head": peer}, device_id_type=MESH)

    seq_peers(greet_seq)
    head_peers(greet_head)

    loads[0].wait()
    loads[1].wait()
    for h in range(heads):
        first = mm(k[span_rows(0), head_cols(h)], v[span_rows(0), head_cols(h)], TN)
        second = mm(k[span_rows(1), head_cols(h)], v[span_rows(1), head_cols(h)], TN)
        intra[h] = first.astype(BF16)
        total[h * DH : (h + 1) * DH, :] = (first + second).astype(BF16)

    pl.semaphore_wait(barrier, shards + members - 2)

    def send_total(peer):
        send(
            total.at[pl.ds(pl.multiple_of(peer * rows, rows), rows)],
            total_in.at[me],
            send_sem.at[0],
            recv_sem.at[0],
            "seq",
            peer,
        )

    seq_peers(send_total)

    def send_cot(peer):
        send(
            cot_in.at[:, pl.ds(pl.multiple_of(peer * width, width), width)],
            cot.at[pl.ds(pl.multiple_of(mine * piece, piece), piece)],
            send_sem.at[1],
            recv_sem.at[1],
            "head",
            peer,
        )

    head_peers(send_cot)
    total_in[me] = total[pl.ds(pl.multiple_of(me * rows, rows), rows), :]

    for copy in loads[2:6]:
        copy.wait()
    x_ids = lax.broadcasted_iota(jnp.int32, (table, toks), 0)
    stacked = []
    for l in range(levels):
        onehot = (idx[l : l + 1, :] == x_ids).astype(F32).astype(BF16)
        high, low = split_two(tab[l])
        stacked.append(mm(high, onehot, NN))
        stacked.append(mm(low, onehot, NN))
    pad = 128 - 2 * heads * levels
    stacked.append(jnp.zeros((pad, toks), F32))
    columns = jnp.transpose(jnp.concatenate(stacked, axis=0)).astype(BF16)
    row_ids = lax.broadcasted_iota(jnp.int32, (128, width), 0)
    col_head = lax.broadcasted_iota(jnp.int32, (128, width), 1) // DH
    for l in range(levels):
        base = 2 * heads * l
        pick = (row_ids == base + col_head) | (row_ids == base + heads + col_head)
        weight[l] = mm(columns, pick.astype(F32).astype(BF16), NN)

    causal = lax.broadcasted_iota(jnp.int32, (CH, CH), 1) <= lax.broadcasted_iota(
        jnp.int32, (CH, CH), 0
    )
    for h in range(heads):
        for i in range(2):
            at = (span_rows(i), head_cols(h))
            score = jnp.where(causal, mm(q[at], k[at], NT), 0.0)
            scores[2 * h + i] = score
            out[0, at[0], at[1]] = mm(score.astype(BF16), v[at], NN)
        out[1, span_rows(0), head_cols(h)] = jnp.zeros((CH, DH), F32)
        out[1, span_rows(1), head_cols(h)] = mm(
            q[span_rows(1), head_cols(h)], intra[h], NN
        )

    drain(total_in.at[0 : shards - 1], recv_sem.at[0])
    sums = [[total_in[c].astype(F32) for c in range(shards)]]
    for place in range(1, bits):
        below = sums[-1]
        sums.append([below[2 * j] + below[2 * j + 1] for j in range(len(below) // 2)])
    for c in range(shards):
        slot = 0
        for place in range(bits):
            if (c >> place) & 1:
                level[c * bits + slot] = sums[place][(c >> place) ^ 1].astype(BF16)
                slot += 1

    def send_level(peer):
        count = ones_in(peer)
        for n in range(1, bits + 1):

            @pl.when(count == n)
            def _():
                send(
                    level.at[pl.ds(peer * bits, n)],
                    level_in.at[pl.ds(me * bits, n)],
                    send_sem.at[2],
                    recv_sem.at[2],
                    "seq",
                    peer,
                )

    seq_peers(send_level)
    level_in[pl.ds(me * bits, bits)] = level[pl.ds(me * bits, bits)]

    loads[6].wait()
    drain(cot.at[0 : toks - piece], recv_sem.at[1])
    for h in range(heads):
        cols = head_cols(h)
        near[:, cols] = weight[0, :, cols] * out[0, :, cols] + weight[1, :, cols] * out[1, :, cols]
        goal[:, cols] = cot[:, cols].astype(F32) * gain[:, cols]
        for i in range(2):
            weighted[2 * h + i] = (
                scores[2 * h + i] * weight[0, span_rows(i), cols]
            ).astype(BF16)

    for n in range(1, bits + 1):

        @pl.when(my_count == n)
        def _():
            drain(level_in.at[0 : (shards - 1) * n], recv_sem.at[2])

    slot = jnp.int32(0)
    slots = []
    for place in range(bits):
        mark = bit_of(me, place)
        slots.append(slot)
        for h in range(heads):

            @pl.when(mark == 1)
            def _():
                for g in range(group):
                    state[h, g * rows : (g + 1) * rows, place * DH : (place + 1) * DH] = level_in[
                        (h * group + g) * bits + slot
                    ]

            @pl.when(mark == 0)
            def _():
                state[h, :, place * DH : (place + 1) * DH] = jnp.zeros((DH, DH), BF16)

        slot = slot + mark

    squares = jnp.zeros((toks, DH), F32)
    crosses = jnp.zeros((toks, DH), F32)
    for h in range(heads):
        cols = head_cols(h)
        far = mm(q[:, cols], state[h], NN)
        value = near[:, cols]
        for place in range(bits):
            part = far[:, place * DH : (place + 1) * DH]
            out[place + 2, :, cols] = part
            value = value + weight[place + 2, :, cols] * part
        value = value.astype(BF16)
        attn[:, cols] = value
        value = value.astype(F32)
        squares = squares + value * value
        crosses = crosses + goal[:, cols] * value
    one_row = jnp.ones((8, DH), BF16)
    for row, part in enumerate((squares, crosses)):
        high, low = split_two(part)
        both = mm(one_row, high, NT) + mm(one_row, low, NT)
        stat[row : row + 1, :] = both[0:1, :]

    def send_stat(peer):
        send(stat, stat_in.at[mine], send_sem.at[3], recv_sem.at[3], "head", peer)

    head_peers(send_stat)
    stat_in[mine] = stat[...]
    drain(stat_in.at[0 : members - 1], recv_sem.at[3])
    both = stat_in[0]
    for m in range(1, members):
        both = both + stat_in[m]
    inv_row = lax.rsqrt(both[0:1, :] * (1.0 / features) + EPSILON)
    mean_row = both[1:2, :] * inv_row * (1.0 / features)
    inv = jnp.transpose(jnp.broadcast_to(inv_row, (DH, toks)))
    mean = jnp.transpose(jnp.broadcast_to(mean_row, (DH, toks)))

    for h in range(heads):
        cols = head_cols(h)
        unit = attn[:, cols].astype(F32) * inv
        grad_h = ((goal[:, cols] - unit * mean) * inv).astype(BF16)
        grad[:, cols] = grad_h
        grad_f = grad_h.astype(F32)
        for place in range(bits):
            scaled[h, :, place * DH : (place + 1) * DH] = (
                weight[place + 2, :, cols] * grad_f
            ).astype(BF16)
        products = mm(q[:, cols], scaled[h], TN)
        for place in range(bits):

            @pl.when(bit_of(me, place) == 1)
            def _():
                for g in range(group):
                    qg[(h * group + g) * bits + slots[place]] = products[
                        g * rows : (g + 1) * rows, place * DH : (place + 1) * DH
                    ].astype(BF16)

    for n in range(1, bits + 1):

        @pl.when(my_count == n)
        def _():
            def send_qg(peer):
                send(
                    qg.at[pl.ds(peer * bits, n)],
                    qg_in.at[pl.ds(me * bits, n)],
                    send_sem.at[4],
                    recv_sem.at[4],
                    "seq",
                    peer,
                )

            seq_peers(send_qg)

    qg_in[pl.ds(me * bits, bits)] = qg[pl.ds(me * bits, bits)]

    lane_ids = lax.broadcasted_iota(jnp.int32, (8, width), 1) // DH
    head_rows = (
        (lax.broadcasted_iota(jnp.int32, (8, width), 0) == lane_ids).astype(F32).astype(BF16)
    )
    grad_all = grad[...].astype(F32)
    for l in range(levels):
        onehot = (idx[l : l + 1, :] == x_ids).astype(F32).astype(BF16)
        high, low = split_two(out[l] * grad_all)
        by_row = mm(onehot, high, NN) + mm(onehot, low, NN)
        high, low = split_two(by_row)
        result = mm(head_rows, high, NT) + mm(head_rows, low, NT)
        tpart[l] = result[0:heads, :]
    for l in range(levels):

        @pl.when(me != l)
        def _():
            send(tpart.at[l], tpart_in.at[me], send_sem.at[7], recv_sem.at[7], "seq", l)

        @pl.when(me == l)
        def _():
            tpart_in[me] = tpart[l]

    for h in range(heads):
        cols = head_cols(h)
        unit = attn[:, cols].astype(F32) * inv
        normed[:, cols] = (unit * gain[:, cols]).astype(BF16)
        gpart[:, cols] = jnp.sum(cot[:, cols].astype(F32) * unit, axis=0, keepdims=True)

    def send_gain(peer):
        send(gpart, gpart_in.at[me], send_sem.at[6], recv_sem.at[6], "seq", peer)

    seq_peers(send_gain)
    gpart_in[me] = gpart[...]

    def send_normed(peer):
        send(
            normed.at[pl.ds(pl.multiple_of(peer * piece, piece), piece)],
            normed_out.at[:, my_cols],
            send_sem.at[5],
            recv_sem.at[5],
            "head",
            peer,
        )

    head_peers(send_normed)
    normed_out[:, my_cols] = normed[pl.ds(pl.multiple_of(mine * piece, piece), piece), :]

    for h in range(heads):
        cols = head_cols(h)
        grad_h = grad[:, cols]
        far = mm(scaled[h], state[h], NT)
        within = (weight[1, span_rows(1), cols] * grad_h[CH:].astype(F32)).astype(BF16)
        inner[h] = mm(q[span_rows(1), cols], within, TN)
        for i in range(2):
            at = (span_rows(i), cols)
            along = mm(grad_h[span_rows(i)], v[at], NT)
            first = weight[0, span_rows(i), cols]
            grad_scores = jnp.where(causal, along * first, 0.0).astype(BF16)
            value = far[span_rows(i)] + mm(grad_scores, k[at], NN)
            if i == 1:
                value = value + mm(within, intra[h], NT)
            dq[at] = value.astype(BF16)
            dk[at] = mm(grad_scores, q[at], TN)
            dv[at] = mm(weighted[2 * h + i], grad_h[span_rows(i)], TN)

    for n in range(0, bits + 1):

        @pl.when(my_count == n)
        def _():
            drain(qg_in.at[0 : bits * shards // 2 - n], recv_sem.at[4])

    def slot_of(c, place):
        return bin(c & ((1 << place) - 1)).count("1")

    reach = [None]
    for place in range(bits - 1, -1, -1):
        reach_next = []
        for block, above in enumerate(reach):
            upper = range((2 * block + 1) << place, (2 * block + 2) << place)
            part = functools.reduce(
                lambda a, b: a + b,
                [qg_in[c * bits + slot_of(c, place)].astype(F32) for c in upper],
            )
            reach_next.append(part if above is None else above + part)
            reach_next.append(above)
        reach = reach_next
    for c in range(shards):
        ks[c] = jnp.zeros((rows, DH), BF16) if reach[c] is None else reach[c].astype(BF16)

    def send_ks(peer):
        send(ks.at[peer], ks_in.at[me], send_sem.at[9], recv_sem.at[9], "seq", peer)

    seq_peers(send_ks)
    ks_in[me] = ks[me]

    drain(gpart_in.at[0 : shards - 1], recv_sem.at[6])
    both = gpart_in[0]
    for c in range(1, shards):
        both = both + gpart_in[c]
    gsum[...] = both

    def send_gsum(peer):
        send(gsum, gall.at[:, my_cols], send_sem.at[8], recv_sem.at[8], "head", peer)

    head_peers(send_gsum)
    gall[:, my_cols] = both

    for l in range(levels):

        @pl.when(me == l)
        def _():
            drain(tpart_in.at[0 : shards - 1], recv_sem.at[7])
            both = tpart_in[0]
            for c in range(1, shards):
                both = both + tpart_in[c]
            tsum[l] = both

            def send_tsum(peer):
                send(tsum.at[l], tsum.at[l], send_sem.at[10], tab_sem.at[l], "seq", peer)

            seq_peers(send_tsum)

    drain(ks_in.at[0 : shards - 1], recv_sem.at[9])
    for h in range(heads):
        cols = head_cols(h)
        cross = ks_in[h * group : (h + 1) * group].reshape(DH, DH)
        for i in range(2):
            at = (span_rows(i), cols)
            key_state = cross
            if i == 0:
                key_state = (cross.astype(F32) + inner[h]).astype(BF16)
            dk_bf[at] = (dk[at] + mm(v[at], key_state, NT)).astype(BF16)
            dv_bf[at] = (dv[at] + mm(k[at], key_state, NN)).astype(BF16)

    drain(gall.at[:, 0 : features - width], recv_sem.at[8])
    for l in range(levels):

        @pl.when(me != l)
        def _():
            drain(tsum.at[l], tab_sem.at[l])

    drain(normed_out.at[:, 0 : features - width], recv_sem.at[5])
    drain(total.at[0 : (shards - 1) * rows], send_sem.at[0])
    drain(cot.at[0 : toks - piece], send_sem.at[1])
    drain(stat_in.at[0 : members - 1], send_sem.at[3])
    for n in range(0, bits + 1):

        @pl.when(my_count == n)
        def _():
            drain(level.at[0 : bits * shards // 2 - n], send_sem.at[2])
            if n:
                drain(qg.at[0 : (shards - 1) * n], send_sem.at[4])

    drain(normed.at[0 : toks - piece], send_sem.at[5])
    drain(gpart_in.at[0 : shards - 1], send_sem.at[6])
    drain(gall.at[:, 0 : features - width], send_sem.at[8])
    drain(ks_in.at[0 : shards - 1], send_sem.at[9])

    @pl.when(me < levels)
    def _():
        drain(tpart.at[0 : levels - 1], send_sem.at[7])
        drain(tpart_in.at[0 : shards - 1], send_sem.at[10])

    @pl.when(me >= levels)
    def _():
        drain(tpart, send_sem.at[7])


def copy_kernel(*refs):
    count = len(refs) // 2
    sems = refs[-1]
    copies = [
        pltpu.make_async_copy(refs[i], refs[count + i], sems.at[i]) for i in range(count)
    ]
    for copy in copies:
        copy.start()
    for copy in copies:
        copy.wait()


def body(shards, members, queries, key_rows, value_rows, level_table, level_index, norm_gain, cotangent):
    toks, width = queries.shape
    table, levels, heads = level_table.shape
    features = norm_gain.shape[0]
    bits = shards.bit_length() - 1
    rows = heads * DH // shards
    anywhere = pl.BlockSpec(memory_space=pl.ANY)
    vmem = pltpu.VMEM
    outs = pl.pallas_call(
        functools.partial(kernel, shards, members),
        out_shape=(
            jax.ShapeDtypeStruct(cotangent.shape, BF16),
            jax.ShapeDtypeStruct((toks, width), BF16),
            jax.ShapeDtypeStruct((toks, width), BF16),
            jax.ShapeDtypeStruct((toks, width), BF16),
            jax.ShapeDtypeStruct((levels, heads, table), F32),
            jax.ShapeDtypeStruct((1, features), F32),
        ),
        in_specs=[anywhere] * 7,
        out_specs=[pl.BlockSpec(memory_space=pltpu.VMEM)] * 6,
        scratch_shapes=[
            vmem((toks, width), BF16),
            vmem((toks, width), BF16),
            vmem((toks, width), BF16),
            vmem((levels, heads, table), F32),
            vmem((levels, toks), jnp.int32),
            vmem((1, width), F32),
            vmem((toks, width), BF16),
            vmem((heads * DH, DH), BF16),
            vmem((shards, rows, DH), BF16),
            vmem((shards * bits, rows, DH), BF16),
            vmem((shards * bits, rows, DH), BF16),
            vmem((heads, DH, bits * DH), BF16),
            vmem((heads, DH, DH), BF16),
            vmem((levels, toks, width), F32),
            vmem((levels, toks, width), F32),
            vmem((2 * heads, CH, CH), F32),
            vmem((toks, width), BF16),
            vmem((2, toks), F32),
            vmem((members, 2, toks), F32),
            vmem((toks, width), BF16),
            vmem((1, width), F32),
            vmem((shards, 1, width), F32),
            vmem((1, width), F32),
            vmem((toks, width), BF16),
            vmem((shards * bits, rows, DH), BF16),
            vmem((shards * bits, rows, DH), BF16),
            vmem((heads, DH, DH), F32),
            vmem((shards, rows, DH), BF16),
            vmem((shards, rows, DH), BF16),
            vmem((toks, width), F32),
            vmem((toks, width), F32),
            vmem((levels, heads, table), F32),
            vmem((shards, heads, table), F32),
            vmem((toks, width), F32),
            vmem((toks, width), F32),
            vmem((2 * heads, CH, CH), BF16),
            vmem((heads, toks, bits * DH), BF16),
            pltpu.SemaphoreType.DMA((7,)),
            pltpu.SemaphoreType.DMA((11,)),
            pltpu.SemaphoreType.DMA((10,)),
            pltpu.SemaphoreType.DMA((levels,)),
        ],
        compiler_params=pltpu.CompilerParams(
            collective_id=0, has_side_effects=True, vmem_limit_bytes=VMEM_BYTES
        ),
    )(
        *(
            pltpu.with_memory_space_constraint(array, pltpu.HBM)
            for array in (
                queries,
                key_rows,
                value_rows,
                jnp.transpose(level_table, (1, 2, 0)),
                jnp.transpose(level_index),
                norm_gain.reshape(1, features),
                cotangent,
            )
        )
    )
    normed, dq, dk, dv, gtab, ggain = pl.pallas_call(
        copy_kernel,
        out_shape=tuple(jax.ShapeDtypeStruct(o.shape, o.dtype) for o in outs),
        in_specs=[pl.BlockSpec(memory_space=pltpu.VMEM)] * 6,
        out_specs=[anywhere] * 6,
        scratch_shapes=[pltpu.SemaphoreType.DMA((6,))],
        compiler_params=pltpu.CompilerParams(vmem_limit_bytes=4 * 2**20),
    )(*outs)
    return normed, dq, dk, dv, jnp.transpose(gtab, (2, 0, 1)), ggain.reshape(features)


def solution(mesh):
    wide = P("seq", "head")
    rows = P(("seq", "head"), None)
    table = P(None, None, "head")
    return jax.shard_map(
        functools.partial(body, mesh.shape["seq"], mesh.shape["head"]),
        mesh=mesh,
        in_specs=(wide, wide, wide, table, P("seq", None), P(), rows),
        out_specs=(rows, wide, wide, wide, table, P()),
        check_vma=False,
    )
```

```python
import functools

import jax
import jax.numpy as jnp
from jax import lax
from jax.experimental import pallas as pl
from jax.experimental.pallas import tpu as pltpu
from jax.sharding import PartitionSpec as P

CH = 128
DH = 128
EPSILON = 1e-06
NX = 4
VMEM_BYTES = 48 * 2**20
MESH = pl.DeviceIdType.MESH
F32 = jnp.float32
BF16 = jnp.bfloat16

NN = (((1,), (0,)), ((), ()))
NT = (((1,), (1,)), ((), ()))
TN = (((0,), (0,)), ((), ()))


def mm(a, b, dims):
    return lax.dot_general(a, b, dims, preferred_element_type=F32)


def split_two(value):
    high = value.astype(BF16)
    low = (value - high.astype(F32)).astype(BF16)
    return high, low


def bit_of(index, place):
    return lax.rem(lax.div(index, jnp.int32(2**place)), jnp.int32(2))


def send(src, dst, send_sem, recv_sem, axis, target):
    pltpu.make_async_remote_copy(
        src_ref=src,
        dst_ref=dst,
        send_sem=send_sem,
        recv_sem=recv_sem,
        device_id={axis: target},
        device_id_type=MESH,
    ).start()


def drain(view, sem):
    pltpu.make_async_copy(view, view, sem).wait()


def kernel(
    shards,
    members,
    q_in,
    k_in,
    v_in,
    tab_in,
    idx_in,
    gain_in,
    cot_in,
    normed_out,
    dq,
    dk_bf,
    dv_bf,
    tsum,
    gall,
    q,
    k,
    v,
    tab,
    idx,
    gain,
    cot,
    total,
    total_in,
    level,
    level_in,
    state,
    intra,
    weight,
    out,
    scores,
    attn,
    stat,
    stat_in,
    normed,
    gpart,
    gpart_in,
    gsum,
    grad,
    qg,
    qg_in,
    inner,
    ks,
    ks_in,
    dk,
    dv,
    tpart,
    tpart_in,
    near,
    goal,
    weighted,
    scaled,
    row_in,
    row_level,
    row_level_in,
    row_qg,
    row_qg_in,
    row_ks,
    row_ks_in,
    gline,
    gline_in,
    load_sem,
    send_sem,
    recv_sem,
    tab_sem,
):
    me = lax.axis_index("seq")
    mine = lax.axis_index("head")
    bits = shards.bit_length() - 1
    far_bits = bits - 2
    lines = shards // NX
    toks, width = q.shape
    heads = width // DH
    levels = bits + 2
    rows = heads * DH // shards
    group = shards // heads
    piece = toks // members
    table = tab.shape[2]
    features = members * width

    def head_cols(h):
        return slice(h * DH, (h + 1) * DH)

    def span_rows(i):
        return slice(i * CH, (i + 1) * CH)

    def from_far(index, count):
        step = lax.rem(index, jnp.int32(2))
        return count // 2 + (1 - 2 * step) * lax.div(index + 1, jnp.int32(2))

    def seq_peers(step):
        def one(index, carry):
            line = lax.div(me, jnp.int32(NX)) + from_far(lax.div(index, jnp.int32(NX)), lines)
            place = lax.rem(me, jnp.int32(NX)) + from_far(lax.rem(index, jnp.int32(NX)), NX)
            step(lax.rem(line, jnp.int32(lines)) * NX + lax.rem(place, jnp.int32(NX)))
            return carry

        lax.fori_loop(0, shards - 1, one, 0)

    def head_peers(step):
        def one(index, carry):
            along = lax.div(mine, jnp.int32(2)) + from_far(lax.div(index, jnp.int32(2)), members // 2)
            core = lax.rem(mine, jnp.int32(2)) + from_far(lax.rem(index, jnp.int32(2)), 2)
            step(lax.rem(along, jnp.int32(members // 2)) * 2 + lax.rem(core, jnp.int32(2)))
            return carry

        lax.fori_loop(0, members - 1, one, 0)

    def ones_in(index):
        count = jnp.int32(0)
        for place in range(2, bits):
            count = count + bit_of(index, place)
        return count

    my_count = ones_in(me)
    across = lax.rem(me, jnp.int32(NX))
    down = lax.div(me, jnp.int32(NX))
    row_count = bit_of(me, 0) + bit_of(me, 1)
    far_slots = far_bits * shards // 2

    def row_peers(step):
        for offset in range(1, NX):
            place = lax.rem(across + offset, jnp.int32(NX))
            step(place, down * NX + place)

    my_cols = pl.ds(pl.multiple_of(mine * width, width), width)

    loads = [
        pltpu.make_async_copy(k_in, k, load_sem.at[0]),
        pltpu.make_async_copy(v_in, v, load_sem.at[1]),
        pltpu.make_async_copy(q_in, q, load_sem.at[2]),
        pltpu.make_async_copy(tab_in, tab, load_sem.at[3]),
        pltpu.make_async_copy(idx_in, idx, load_sem.at[4]),
        pltpu.make_async_copy(gain_in.at[:, my_cols], gain, load_sem.at[5]),
        pltpu.make_async_copy(
            cot_in.at[:, my_cols],
            cot.at[pl.ds(pl.multiple_of(mine * piece, piece), piece)],
            load_sem.at[6],
        ),
    ]
    for copy in loads:
        copy.start()

    barrier = pltpu.get_barrier_semaphore()

    def greet_seq(offset, carry):
        peer = lax.rem(me + offset, jnp.int32(shards))
        pl.semaphore_signal(barrier, inc=1, device_id={"seq": peer}, device_id_type=MESH)
        return carry

    def greet_head(offset, carry):
        peer = lax.rem(mine + offset, jnp.int32(members))
        pl.semaphore_signal(barrier, inc=1, device_id={"head": peer}, device_id_type=MESH)
        return carry

    lax.fori_loop(1, shards, greet_seq, 0)
    lax.fori_loop(1, members, greet_head, 0)

    loads[0].wait()
    loads[1].wait()
    for h in range(heads):
        first = mm(k[span_rows(0), head_cols(h)], v[span_rows(0), head_cols(h)], TN)
        second = mm(k[span_rows(1), head_cols(h)], v[span_rows(1), head_cols(h)], TN)
        intra[h] = first.astype(BF16)
        total[h * DH : (h + 1) * DH, :] = (first + second).astype(BF16)

    pl.semaphore_wait(barrier, shards + members - 2)

    def send_total(peer):
        send(
            total.at[pl.ds(pl.multiple_of(peer * rows, rows), rows)],
            total_in.at[me],
            send_sem.at[0],
            recv_sem.at[0],
            "seq",
            peer,
        )

    seq_peers(send_total)

    def send_row(place, peer):
        send(
            total.at[pl.ds(pl.multiple_of(place * DH, DH), DH)],
            row_in.at[across],
            send_sem.at[11],
            recv_sem.at[11],
            "seq",
            peer,
        )

    row_peers(send_row)

    def send_cot(peer):
        send(
            cot_in.at[:, pl.ds(pl.multiple_of(peer * width, width), width)],
            cot.at[pl.ds(pl.multiple_of(mine * piece, piece), piece)],
            send_sem.at[1],
            recv_sem.at[1],
            "head",
            peer,
        )

    head_peers(send_cot)
    total_in[me] = total[pl.ds(pl.multiple_of(me * rows, rows), rows), :]
    row_in[across] = total[pl.ds(pl.multiple_of(across * DH, DH), DH), :]

    for copy in loads[2:6]:
        copy.wait()
    x_ids = lax.broadcasted_iota(jnp.int32, (table, toks), 0)
    stacked = []
    for l in range(levels):
        onehot = (idx[l : l + 1, :] == x_ids).astype(F32).astype(BF16)
        high, low = split_two(tab[l])
        stacked.append(mm(high, onehot, NN))
        stacked.append(mm(low, onehot, NN))
    pad = 128 - 2 * heads * levels
    stacked.append(jnp.zeros((pad, toks), F32))
    columns = jnp.transpose(jnp.concatenate(stacked, axis=0)).astype(BF16)
    row_ids = lax.broadcasted_iota(jnp.int32, (128, width), 0)
    col_head = lax.broadcasted_iota(jnp.int32, (128, width), 1) // DH
    for l in range(levels):
        base = 2 * heads * l
        pick = (row_ids == base + col_head) | (row_ids == base + heads + col_head)
        weight[l] = mm(columns, pick.astype(F32).astype(BF16), NN)

    causal = lax.broadcasted_iota(jnp.int32, (CH, CH), 1) <= lax.broadcasted_iota(
        jnp.int32, (CH, CH), 0
    )
    for h in range(heads):
        for i in range(2):
            at = (span_rows(i), head_cols(h))
            score = jnp.where(causal, mm(q[at], k[at], NT), 0.0)
            scores[2 * h + i] = score
            out[0, at[0], at[1]] = mm(score.astype(BF16), v[at], NN)
        out[1, span_rows(0), head_cols(h)] = jnp.zeros((CH, DH), F32)
        out[1, span_rows(1), head_cols(h)] = mm(
            q[span_rows(1), head_cols(h)], intra[h], NN
        )

    drain(total_in.at[0 : shards - 1], recv_sem.at[0])
    sums = [
        functools.reduce(
            lambda a, b: a + b,
            [total_in[NX * line + place].astype(F32) for place in range(NX)],
        )
        for line in range(lines)
    ]
    sums = [sums]
    for place in range(1, far_bits):
        below = sums[-1]
        sums.append([below[2 * j] + below[2 * j + 1] for j in range(len(below) // 2)])
    for line in range(lines):
        slot = 0
        for place in range(far_bits):
            if (line >> place) & 1:
                block = sums[place][(line >> place) ^ 1].astype(BF16)
                for c in range(NX * line, NX * line + NX):
                    level[c * far_bits + slot] = block
                slot += 1

    def send_level(peer):
        count = ones_in(peer)
        for n in range(1, far_bits + 1):

            @pl.when(count == n)
            def _():
                send(
                    level.at[pl.ds(peer * far_bits, n)],
                    level_in.at[pl.ds(me * far_bits, n)],
                    send_sem.at[2],
                    recv_sem.at[2],
                    "seq",
                    peer,
                )

    seq_peers(send_level)
    level_in[pl.ds(me * far_bits, far_bits)] = level[pl.ds(me * far_bits, far_bits)]

    drain(row_in.at[0 : NX - 1], recv_sem.at[11])
    pair = (row_in[0].astype(F32) + row_in[1].astype(F32)).astype(BF16)
    row_level[2] = row_in[0]
    row_level[4] = pair
    row_level[6] = row_in[2]
    row_level[7] = pair
    for place in range(1, NX):
        n = bin(place).count("1")

        @pl.when(across != place)
        def _():
            send(
                row_level.at[2 * place : 2 * place + n],
                row_level_in.at[pl.ds(2 * across, n)],
                send_sem.at[12],
                recv_sem.at[12],
                "seq",
                down * NX + place,
            )

        @pl.when(across == place)
        def _():
            row_level_in[2 * place : 2 * place + n] = row_level[2 * place : 2 * place + n]

    loads[6].wait()
    drain(cot.at[0 : toks - piece], recv_sem.at[1])
    for h in range(heads):
        cols = head_cols(h)
        near[:, cols] = weight[0, :, cols] * out[0, :, cols] + weight[1, :, cols] * out[1, :, cols]
        goal[:, cols] = cot[:, cols].astype(F32) * gain[:, cols]
        for i in range(2):
            weighted[2 * h + i] = (
                scores[2 * h + i] * weight[0, span_rows(i), cols]
            ).astype(BF16)

    for n in range(1, far_bits + 1):

        @pl.when(my_count == n)
        def _():
            drain(level_in.at[0 : (shards - 1) * n], recv_sem.at[2])

    for n in (1, 2):

        @pl.when(row_count == n)
        def _():
            drain(row_level_in.at[0 : (NX - 1) * n], recv_sem.at[12])

    slots = []
    for place in range(bits):
        if place in (0, 2):
            slot = jnp.int32(0)
        mark = bit_of(me, place)
        slots.append(slot)
        lanes = slice(place * DH, (place + 1) * DH)
        for h in range(heads):

            @pl.when(mark == 1)
            def _():
                if place < 2:
                    state[h, :, lanes] = row_level_in[2 * h + slot]
                else:
                    for g in range(group):
                        state[h, g * rows : (g + 1) * rows, lanes] = level_in[
                            (h * group + g) * far_bits + slot
                        ]

            @pl.when(mark == 0)
            def _():
                state[h, :, lanes] = jnp.zeros((DH, DH), BF16)

        slot = slot + mark

    squares = jnp.zeros((toks, DH), F32)
    crosses = jnp.zeros((toks, DH), F32)
    for h in range(heads):
        cols = head_cols(h)
        far = mm(q[:, cols], state[h], NN)
        value = near[:, cols]
        for place in range(bits):
            part = far[:, place * DH : (place + 1) * DH]
            out[place + 2, :, cols] = part
            value = value + weight[place + 2, :, cols] * part
        value = value.astype(BF16)
        attn[:, cols] = value
        value = value.astype(F32)
        squares = squares + value * value
        crosses = crosses + goal[:, cols] * value
    one_row = jnp.ones((8, DH), BF16)
    for row, part in enumerate((squares, crosses)):
        high, low = split_two(part)
        both = mm(one_row, high, NT) + mm(one_row, low, NT)
        stat[row : row + 1, :] = both[0:1, :]

    def send_stat(peer):
        send(stat, stat_in.at[mine], send_sem.at[3], recv_sem.at[3], "head", peer)

    head_peers(send_stat)
    stat_in[mine] = stat[...]
    drain(stat_in.at[0 : members - 1], recv_sem.at[3])
    both = stat_in[0]
    for m in range(1, members):
        both = both + stat_in[m]
    inv_row = lax.rsqrt(both[0:1, :] * (1.0 / features) + EPSILON)
    mean_row = both[1:2, :] * inv_row * (1.0 / features)
    inv = jnp.transpose(jnp.broadcast_to(inv_row, (DH, toks)))
    mean = jnp.transpose(jnp.broadcast_to(mean_row, (DH, toks)))

    for h in range(heads):
        cols = head_cols(h)
        unit = attn[:, cols].astype(F32) * inv
        grad_h = ((goal[:, cols] - unit * mean) * inv).astype(BF16)
        grad[:, cols] = grad_h
        grad_f = grad_h.astype(F32)
        for place in range(bits):
            scaled[h, :, place * DH : (place + 1) * DH] = (
                weight[place + 2, :, cols] * grad_f
            ).astype(BF16)
        products = mm(q[:, cols], scaled[h], TN)
        for place in range(bits):

            @pl.when(bit_of(me, place) == 1)
            def _():
                part = products[:, place * DH : (place + 1) * DH].astype(BF16)
                if place < 2:
                    row_qg[2 * h + slots[place]] = part
                else:
                    for g in range(group):
                        qg[(h * group + g) * far_bits + slots[place]] = part[
                            g * rows : (g + 1) * rows
                        ]

    for n in range(1, far_bits + 1):

        @pl.when(my_count == n)
        def _():
            def send_qg(peer):
                send(
                    qg.at[pl.ds(peer * far_bits, n)],
                    qg_in.at[pl.ds(me * far_bits, n)],
                    send_sem.at[4],
                    recv_sem.at[4],
                    "seq",
                    peer,
                )

            seq_peers(send_qg)

    qg_in[pl.ds(me * far_bits, far_bits)] = qg[pl.ds(me * far_bits, far_bits)]
    for n in (1, 2):

        @pl.when(row_count == n)
        def _():
            def send_row_qg(place, peer):
                send(
                    row_qg.at[pl.ds(2 * place, n)],
                    row_qg_in.at[pl.ds(2 * across, n)],
                    send_sem.at[13],
                    recv_sem.at[13],
                    "seq",
                    peer,
                )

            row_peers(send_row_qg)
            row_qg_in[pl.ds(2 * across, n)] = row_qg[pl.ds(2 * across, n)]

    lane_ids = lax.broadcasted_iota(jnp.int32, (8, width), 1) // DH
    head_rows = (
        (lax.broadcasted_iota(jnp.int32, (8, width), 0) == lane_ids).astype(F32).astype(BF16)
    )
    grad_all = grad[...].astype(F32)
    for l in range(levels):
        onehot = (idx[l : l + 1, :] == x_ids).astype(F32).astype(BF16)
        high, low = split_two(out[l] * grad_all)
        by_row = mm(onehot, high, NN) + mm(onehot, low, NN)
        high, low = split_two(by_row)
        result = mm(head_rows, high, NT) + mm(head_rows, low, NT)
        tpart[l] = result[0:heads, :]
    for l in range(levels):

        @pl.when(me != l)
        def _():
            send(tpart.at[l], tpart_in.at[me], send_sem.at[7], recv_sem.at[7], "seq", l)

        @pl.when(me == l)
        def _():
            tpart_in[me] = tpart[l]

    for h in range(heads):
        cols = head_cols(h)
        unit = attn[:, cols].astype(F32) * inv
        normed[:, cols] = (unit * gain[:, cols]).astype(BF16)
        gpart[:, cols] = jnp.sum(cot[:, cols].astype(F32) * unit, axis=0, keepdims=True)

    def send_gain(place, peer):
        send(gpart, gpart_in.at[across], send_sem.at[6], recv_sem.at[6], "seq", peer)

    row_peers(send_gain)
    gpart_in[across] = gpart[...]

    def send_normed(peer):
        send(
            normed.at[pl.ds(pl.multiple_of(peer * piece, piece), piece)],
            normed_out.at[:, my_cols],
            send_sem.at[5],
            recv_sem.at[5],
            "head",
            peer,
        )

    head_peers(send_normed)
    normed_out[:, my_cols] = normed[pl.ds(pl.multiple_of(mine * piece, piece), piece), :]

    for h in range(heads):
        cols = head_cols(h)
        grad_h = grad[:, cols]
        far = mm(scaled[h], state[h], NT)
        within = (weight[1, span_rows(1), cols] * grad_h[CH:].astype(F32)).astype(BF16)
        inner[h] = mm(q[span_rows(1), cols], within, TN)
        for i in range(2):
            at = (span_rows(i), cols)
            along = mm(grad_h[span_rows(i)], v[at], NT)
            first = weight[0, span_rows(i), cols]
            grad_scores = jnp.where(causal, along * first, 0.0).astype(BF16)
            value = far[span_rows(i)] + mm(grad_scores, k[at], NN)
            if i == 1:
                value = value + mm(within, intra[h], NT)
            dq[at] = value.astype(BF16)
            dk[at] = mm(grad_scores, q[at], TN)
            dv[at] = mm(weighted[2 * h + i], grad_h[span_rows(i)], TN)

    drain(gpart_in.at[0 : NX - 1], recv_sem.at[6])
    both = gpart_in[0]
    for c in range(1, NX):
        both = both + gpart_in[c]
    gline[...] = both
    gline_in[down] = both
    for offset in range(1, lines):
        line = lax.rem(down + offset, jnp.int32(lines))
        send(
            gline,
            gline_in.at[down],
            send_sem.at[14],
            recv_sem.at[14],
            "seq",
            line * NX + across,
        )

    for n in range(0, far_bits + 1):

        @pl.when(my_count == n)
        def _():
            drain(qg_in.at[0 : far_slots - n], recv_sem.at[4])

    def slot_of(line, place):
        return bin(line & ((1 << place) - 1)).count("1")

    reach = [None]
    for place in range(far_bits - 1, -1, -1):
        reach_next = []
        for block, above in enumerate(reach):
            upper = range((2 * block + 1) << place, (2 * block + 2) << place)
            part = functools.reduce(
                lambda a, b: a + b,
                [
                    qg_in[c * far_bits + slot_of(line, place)].astype(F32)
                    for line in upper
                    for c in range(NX * line, NX * line + NX)
                ],
            )
            reach_next.append(part if above is None else above + part)
            reach_next.append(above)
        reach = reach_next
    for line in range(lines):
        block = jnp.zeros((rows, DH), BF16) if reach[line] is None else reach[line].astype(BF16)
        for c in range(NX * line, NX * line + NX):
            ks[c] = block

    def send_ks(peer):
        send(ks.at[peer], ks_in.at[me], send_sem.at[9], recv_sem.at[9], "seq", peer)

    seq_peers(send_ks)
    ks_in[me] = ks[me]

    for n in (0, 1, 2):

        @pl.when(row_count == n)
        def _():
            drain(row_qg_in.at[0 : NX - n], recv_sem.at[13])

    both = row_qg_in[4].astype(F32) + row_qg_in[7].astype(F32)
    row_ks[0] = (row_qg_in[2].astype(F32) + both).astype(BF16)
    row_ks[1] = both.astype(BF16)
    row_ks[2] = row_qg_in[6]
    row_ks[3] = jnp.zeros((DH, DH), BF16)
    row_ks_in[across] = row_ks[across]
    for place in range(NX - 1):

        @pl.when(across != place)
        def _():
            send(
                row_ks.at[place],
                row_ks_in.at[across],
                send_sem.at[15],
                recv_sem.at[15],
                "seq",
                down * NX + place,
            )

    @pl.when(across == NX - 1)
    def _():
        for place in range(NX - 1):
            row_ks_in[place] = jnp.zeros((DH, DH), BF16)

    if lines > 1:
        drain(gline_in.at[0 : lines - 1], recv_sem.at[14])
    both = gline_in[0]
    for c in range(1, lines):
        both = both + gline_in[c]
    gsum[...] = both

    def send_gsum(peer):
        send(gsum, gall.at[:, my_cols], send_sem.at[8], recv_sem.at[8], "head", peer)

    head_peers(send_gsum)
    gall[:, my_cols] = both

    for l in range(levels):

        @pl.when(me == l)
        def _():
            drain(tpart_in.at[0 : shards - 1], recv_sem.at[7])
            both = tpart_in[0]
            for c in range(1, shards):
                both = both + tpart_in[c]
            tsum[l] = both

            def send_tsum(peer):
                send(tsum.at[l], tsum.at[l], send_sem.at[10], tab_sem.at[l], "seq", peer)

            seq_peers(send_tsum)

    drain(ks_in.at[0 : shards - 1], recv_sem.at[9])

    @pl.when(across != NX - 1)
    def _():
        drain(row_ks_in.at[0 : NX - 1], recv_sem.at[15])

    for h in range(heads):
        cols = head_cols(h)
        cross = ks_in[h * group : (h + 1) * group].reshape(DH, DH).astype(F32)
        cross = cross + row_ks_in[h].astype(F32)
        for i in range(2):
            at = (span_rows(i), cols)
            key_state = (cross + inner[h] if i == 0 else cross).astype(BF16)
            dk_bf[at] = (dk[at] + mm(v[at], key_state, NT)).astype(BF16)
            dv_bf[at] = (dv[at] + mm(k[at], key_state, NN)).astype(BF16)

    drain(gall.at[:, 0 : features - width], recv_sem.at[8])
    for l in range(levels):

        @pl.when(me != l)
        def _():
            drain(tsum.at[l], tab_sem.at[l])

    drain(normed_out.at[:, 0 : features - width], recv_sem.at[5])
    drain(total.at[0 : (shards - 1) * rows], send_sem.at[0])
    drain(cot.at[0 : toks - piece], send_sem.at[1])
    drain(stat_in.at[0 : members - 1], send_sem.at[3])
    for n in range(0, far_bits + 1):

        @pl.when(my_count == n)
        def _():
            drain(level.at[0 : far_slots - n], send_sem.at[2])
            if n:
                drain(qg.at[0 : (shards - 1) * n], send_sem.at[4])

    drain(row_in.at[0 : NX - 1], send_sem.at[11])
    for n in (0, 1, 2):

        @pl.when(row_count == n)
        def _():
            drain(row_level.at[0 : NX - n], send_sem.at[12])
            if n:
                drain(row_qg.at[0 : (NX - 1) * n], send_sem.at[13])

    @pl.when(across == NX - 1)
    def _():
        drain(row_ks.at[0 : NX - 1], send_sem.at[15])

    @pl.when(across != NX - 1)
    def _():
        drain(row_ks.at[0 : NX - 2], send_sem.at[15])

    if lines > 1:
        drain(gline_in.at[0 : lines - 1], send_sem.at[14])
    drain(normed.at[0 : toks - piece], send_sem.at[5])
    drain(gpart_in.at[0 : NX - 1], send_sem.at[6])
    drain(gall.at[:, 0 : features - width], send_sem.at[8])
    drain(ks_in.at[0 : shards - 1], send_sem.at[9])

    @pl.when(me < levels)
    def _():
        drain(tpart.at[0 : levels - 1], send_sem.at[7])
        drain(tpart_in.at[0 : shards - 1], send_sem.at[10])

    @pl.when(me >= levels)
    def _():
        drain(tpart, send_sem.at[7])


def copy_kernel(*refs):
    count = len(refs) // 2
    sems = refs[-1]
    copies = [
        pltpu.make_async_copy(refs[i], refs[count + i], sems.at[i]) for i in range(count)
    ]
    for copy in copies:
        copy.start()
    for copy in copies:
        copy.wait()


def body(shards, members, queries, key_rows, value_rows, level_table, level_index, norm_gain, cotangent):
    toks, width = queries.shape
    table, levels, heads = level_table.shape
    features = norm_gain.shape[0]
    bits = shards.bit_length() - 1
    rows = heads * DH // shards
    anywhere = pl.BlockSpec(memory_space=pl.ANY)
    vmem = pltpu.VMEM
    outs = pl.pallas_call(
        functools.partial(kernel, shards, members),
        out_shape=(
            jax.ShapeDtypeStruct(cotangent.shape, BF16),
            jax.ShapeDtypeStruct((toks, width), BF16),
            jax.ShapeDtypeStruct((toks, width), BF16),
            jax.ShapeDtypeStruct((toks, width), BF16),
            jax.ShapeDtypeStruct((levels, heads, table), F32),
            jax.ShapeDtypeStruct((1, features), F32),
        ),
        in_specs=[anywhere] * 7,
        out_specs=[pl.BlockSpec(memory_space=pltpu.VMEM)] * 6,
        scratch_shapes=[
            vmem((toks, width), BF16),
            vmem((toks, width), BF16),
            vmem((toks, width), BF16),
            vmem((levels, heads, table), F32),
            vmem((levels, toks), jnp.int32),
            vmem((1, width), F32),
            vmem((toks, width), BF16),
            vmem((heads * DH, DH), BF16),
            vmem((shards, rows, DH), BF16),
            vmem((shards * (bits - 2), rows, DH), BF16),
            vmem((shards * (bits - 2), rows, DH), BF16),
            vmem((heads, DH, bits * DH), BF16),
            vmem((heads, DH, DH), BF16),
            vmem((levels, toks, width), F32),
            vmem((levels, toks, width), F32),
            vmem((2 * heads, CH, CH), F32),
            vmem((toks, width), BF16),
            vmem((2, toks), F32),
            vmem((members, 2, toks), F32),
            vmem((toks, width), BF16),
            vmem((1, width), F32),
            vmem((NX, 1, width), F32),
            vmem((1, width), F32),
            vmem((toks, width), BF16),
            vmem((shards * (bits - 2), rows, DH), BF16),
            vmem((shards * (bits - 2), rows, DH), BF16),
            vmem((heads, DH, DH), F32),
            vmem((shards, rows, DH), BF16),
            vmem((shards, rows, DH), BF16),
            vmem((toks, width), F32),
            vmem((toks, width), F32),
            vmem((levels, heads, table), F32),
            vmem((shards, heads, table), F32),
            vmem((toks, width), F32),
            vmem((toks, width), F32),
            vmem((2 * heads, CH, CH), BF16),
            vmem((heads, toks, bits * DH), BF16),
            vmem((NX, DH, DH), BF16),
            vmem((2 * NX, DH, DH), BF16),
            vmem((2 * NX, DH, DH), BF16),
            vmem((2 * NX, DH, DH), BF16),
            vmem((2 * NX, DH, DH), BF16),
            vmem((NX, DH, DH), BF16),
            vmem((NX, DH, DH), BF16),
            vmem((1, width), F32),
            vmem((shards // NX, 1, width), F32),
            pltpu.SemaphoreType.DMA((7,)),
            pltpu.SemaphoreType.DMA((16,)),
            pltpu.SemaphoreType.DMA((16,)),
            pltpu.SemaphoreType.DMA((levels,)),
        ],
        compiler_params=pltpu.CompilerParams(
            collective_id=0, has_side_effects=True, vmem_limit_bytes=VMEM_BYTES
        ),
    )(
        *(
            pltpu.with_memory_space_constraint(array, pltpu.HBM)
            for array in (
                queries,
                key_rows,
                value_rows,
                jnp.transpose(level_table, (1, 2, 0)),
                jnp.transpose(level_index),
                norm_gain.reshape(1, features),
                cotangent,
            )
        )
    )
    normed, dq, dk, dv, gtab, ggain = pl.pallas_call(
        copy_kernel,
        out_shape=tuple(jax.ShapeDtypeStruct(o.shape, o.dtype) for o in outs),
        in_specs=[pl.BlockSpec(memory_space=pltpu.VMEM)] * 6,
        out_specs=[anywhere] * 6,
        scratch_shapes=[pltpu.SemaphoreType.DMA((6,))],
        compiler_params=pltpu.CompilerParams(vmem_limit_bytes=4 * 2**20),
    )(*outs)
    return normed, dq, dk, dv, jnp.transpose(gtab, (2, 0, 1)), ggain.reshape(features)


def solution(mesh):
    wide = P("seq", "head")
    rows = P(("seq", "head"), None)
    table = P(None, None, "head")
    return jax.shard_map(
        functools.partial(body, mesh.shape["seq"], mesh.shape["head"]),
        mesh=mesh,
        in_specs=(wide, wide, wide, table, P("seq", None), P(), rows),
        out_specs=(rows, wide, wide, wide, table, P()),
        check_vma=False,
    )
```

```python
import functools

import jax
import jax.numpy as jnp
from jax import lax
from jax.experimental import pallas as pl
from jax.experimental.pallas import tpu as pltpu
from jax.sharding import PartitionSpec as P

CH = 128
DH = 128
EPSILON = 1e-06
NX = 4
VMEM_BYTES = 48 * 2**20
MESH = pl.DeviceIdType.MESH
F32 = jnp.float32
BF16 = jnp.bfloat16

NN = (((1,), (0,)), ((), ()))
NT = (((1,), (1,)), ((), ()))
TN = (((0,), (0,)), ((), ()))


def mm(a, b, dims):
    return lax.dot_general(a, b, dims, preferred_element_type=F32)


def split_two(value):
    high = value.astype(BF16)
    low = (value - high.astype(F32)).astype(BF16)
    return high, low


def bit_of(index, place):
    return lax.rem(lax.div(index, jnp.int32(2**place)), jnp.int32(2))


def send(src, dst, send_sem, recv_sem, axis, target):
    pltpu.make_async_remote_copy(
        src_ref=src,
        dst_ref=dst,
        send_sem=send_sem,
        recv_sem=recv_sem,
        device_id={axis: target},
        device_id_type=MESH,
    ).start()


def drain(view, sem):
    pltpu.make_async_copy(view, view, sem).wait()


def kernel(
    shards,
    members,
    q_in,
    k_in,
    v_in,
    tab_in,
    idx_in,
    gain_in,
    cot_in,
    normed_out,
    dq,
    dk_bf,
    dv_bf,
    tsum,
    gall,
    q,
    k,
    v,
    tab,
    idx,
    gain,
    cot,
    total,
    total_in,
    level,
    level_in,
    state,
    intra,
    weight,
    out,
    scores,
    attn,
    stat,
    stat_in,
    normed,
    gpart,
    gpart_in,
    gsum,
    grad,
    qg,
    qg_in,
    inner,
    ks,
    ks_in,
    dk,
    dv,
    tpart,
    tpart_in,
    near,
    goal,
    weighted,
    scaled,
    row_in,
    row_level,
    row_level_in,
    row_qg,
    row_qg_in,
    row_ks,
    row_ks_in,
    gline,
    gline_in,
    q_turned,
    load_sem,
    send_sem,
    recv_sem,
    tab_sem,
):
    me = lax.axis_index("seq")
    mine = lax.axis_index("head")
    bits = shards.bit_length() - 1
    far_bits = bits - 2
    lines = shards // NX
    toks, width = q.shape
    heads = width // DH
    levels = bits + 2
    rows = heads * DH // shards
    group = shards // heads
    piece = toks // members
    table = tab.shape[2]
    features = members * width

    def head_cols(h):
        return slice(h * DH, (h + 1) * DH)

    def span_rows(i):
        return slice(i * CH, (i + 1) * CH)

    def from_far(index, count):
        step = lax.rem(index, jnp.int32(2))
        return count // 2 + (1 - 2 * step) * lax.div(index + 1, jnp.int32(2))

    def seq_peers(step):
        def one(index, carry):
            line = lax.div(me, jnp.int32(NX)) + from_far(lax.div(index, jnp.int32(NX)), lines)
            place = lax.rem(me, jnp.int32(NX)) + from_far(lax.rem(index, jnp.int32(NX)), NX)
            step(lax.rem(line, jnp.int32(lines)) * NX + lax.rem(place, jnp.int32(NX)))
            return carry

        lax.fori_loop(0, shards - 1, one, 0)

    def head_peers(step):
        def one(index, carry):
            along = lax.div(mine, jnp.int32(2)) + from_far(lax.div(index, jnp.int32(2)), members // 2)
            core = lax.rem(mine, jnp.int32(2)) + from_far(lax.rem(index, jnp.int32(2)), 2)
            step(lax.rem(along, jnp.int32(members // 2)) * 2 + lax.rem(core, jnp.int32(2)))
            return carry

        lax.fori_loop(0, members - 1, one, 0)

    def ones_in(index):
        count = jnp.int32(0)
        for place in range(2, bits):
            count = count + bit_of(index, place)
        return count

    my_count = ones_in(me)
    across = lax.rem(me, jnp.int32(NX))
    down = lax.div(me, jnp.int32(NX))
    row_count = bit_of(me, 0) + bit_of(me, 1)
    far_slots = far_bits * shards // 2
    owner = [(NX + 1) * l % shards for l in range(levels)]

    def row_peers(step):
        for offset in range(1, NX):
            place = lax.rem(across + offset, jnp.int32(NX))
            step(place, down * NX + place)

    my_cols = pl.ds(pl.multiple_of(mine * width, width), width)

    loads = [
        pltpu.make_async_copy(k_in, k, load_sem.at[0]),
        pltpu.make_async_copy(v_in, v, load_sem.at[1]),
        pltpu.make_async_copy(q_in, q, load_sem.at[2]),
        pltpu.make_async_copy(tab_in, tab, load_sem.at[3]),
        pltpu.make_async_copy(idx_in, idx, load_sem.at[4]),
        pltpu.make_async_copy(gain_in.at[:, my_cols], gain, load_sem.at[5]),
        pltpu.make_async_copy(
            cot_in.at[:, my_cols],
            cot.at[pl.ds(pl.multiple_of(mine * piece, piece), piece)],
            load_sem.at[6],
        ),
    ]
    for copy in loads:
        copy.start()

    barrier = pltpu.get_barrier_semaphore()

    def greet_seq(offset, carry):
        peer = lax.rem(me + offset, jnp.int32(shards))
        pl.semaphore_signal(barrier, inc=1, device_id={"seq": peer}, device_id_type=MESH)
        return carry

    def greet_head(offset, carry):
        peer = lax.rem(mine + offset, jnp.int32(members))
        pl.semaphore_signal(barrier, inc=1, device_id={"head": peer}, device_id_type=MESH)
        return carry

    lax.fori_loop(1, shards, greet_seq, 0)
    lax.fori_loop(1, members, greet_head, 0)

    loads[0].wait()
    loads[1].wait()
    for h in range(heads):
        first = mm(k[span_rows(0), head_cols(h)], v[span_rows(0), head_cols(h)], TN)
        second = mm(k[span_rows(1), head_cols(h)], v[span_rows(1), head_cols(h)], TN)
        intra[h] = first.astype(BF16)
        total[h * DH : (h + 1) * DH, :] = (first + second).astype(BF16)

    pl.semaphore_wait(barrier, shards + members - 2)

    def send_total(peer):
        send(
            total.at[pl.ds(pl.multiple_of(peer * rows, rows), rows)],
            total_in.at[me],
            send_sem.at[0],
            recv_sem.at[0],
            "seq",
            peer,
        )

    seq_peers(send_total)

    def send_row(place, peer):
        send(
            total.at[pl.ds(pl.multiple_of(place * DH, DH), DH)],
            row_in.at[across],
            send_sem.at[11],
            recv_sem.at[11],
            "seq",
            peer,
        )

    row_peers(send_row)

    def send_cot(peer):
        send(
            cot_in.at[:, pl.ds(pl.multiple_of(peer * width, width), width)],
            cot.at[pl.ds(pl.multiple_of(mine * piece, piece), piece)],
            send_sem.at[1],
            recv_sem.at[1],
            "head",
            peer,
        )

    head_peers(send_cot)
    total_in[me] = total[pl.ds(pl.multiple_of(me * rows, rows), rows), :]
    row_in[across] = total[pl.ds(pl.multiple_of(across * DH, DH), DH), :]

    for copy in loads[2:6]:
        copy.wait()
    x_ids = lax.broadcasted_iota(jnp.int32, (table, toks), 0)
    stacked = []
    for l in range(levels):
        onehot = (idx[l : l + 1, :] == x_ids).astype(F32).astype(BF16)
        high, low = split_two(tab[l])
        stacked.append(mm(high, onehot, NN))
        stacked.append(mm(low, onehot, NN))
    pad = 128 - 2 * heads * levels
    stacked.append(jnp.zeros((pad, toks), F32))
    columns = jnp.transpose(jnp.concatenate(stacked, axis=0)).astype(BF16)
    row_ids = lax.broadcasted_iota(jnp.int32, (128, width), 0)
    col_head = lax.broadcasted_iota(jnp.int32, (128, width), 1) // DH
    for l in range(levels):
        base = 2 * heads * l
        pick = (row_ids == base + col_head) | (row_ids == base + heads + col_head)
        weight[l] = mm(columns, pick.astype(F32).astype(BF16), NN)

    causal = lax.broadcasted_iota(jnp.int32, (CH, CH), 1) <= lax.broadcasted_iota(
        jnp.int32, (CH, CH), 0
    )
    for h in range(heads):
        for i in range(2):
            at = (span_rows(i), head_cols(h))
            score = jnp.where(causal, mm(q[at], k[at], NT), 0.0)
            scores[2 * h + i] = score
            out[0, at[0], at[1]] = mm(score.astype(BF16), v[at], NN)
        out[1, span_rows(0), head_cols(h)] = jnp.zeros((CH, DH), F32)
        out[1, span_rows(1), head_cols(h)] = mm(
            q[span_rows(1), head_cols(h)], intra[h], NN
        )

    drain(total_in.at[0 : shards - 1], recv_sem.at[0])
    sums = [
        functools.reduce(
            lambda a, b: a + b,
            [total_in[NX * line + place].astype(F32) for place in range(NX)],
        )
        for line in range(lines)
    ]
    sums = [sums]
    for place in range(1, far_bits):
        below = sums[-1]
        sums.append([below[2 * j] + below[2 * j + 1] for j in range(len(below) // 2)])
    for line in range(lines):
        slot = 0
        for place in range(far_bits):
            if (line >> place) & 1:
                block = sums[place][(line >> place) ^ 1].astype(BF16)
                for c in range(NX * line, NX * line + NX):
                    level[c * far_bits + slot] = block
                slot += 1

    def send_line(index, places):
        line = lax.rem(down + from_far(index, lines), jnp.int32(lines))
        count = ones_in(line * NX)
        for n in range(1, far_bits + 1):

            @pl.when(count == n)
            def _():
                for i in range(places):
                    step = 2 - (i + 1) // 2 if i % 2 else 2 + i // 2
                    peer = line * NX + lax.rem(across + step, jnp.int32(NX))
                    send(
                        level.at[pl.ds(peer * far_bits, n)],
                        level_in.at[pl.ds(me * far_bits, n)],
                        send_sem.at[2],
                        recv_sem.at[2],
                        "seq",
                        peer,
                    )

    def whole_line(index, carry):
        send_line(index, NX)
        return carry

    lax.fori_loop(0, lines - 1, whole_line, 0)
    send_line(jnp.int32(lines - 1), NX - 1)
    level_in[pl.ds(me * far_bits, far_bits)] = level[pl.ds(me * far_bits, far_bits)]

    drain(row_in.at[0 : NX - 1], recv_sem.at[11])
    pair = (row_in[0].astype(F32) + row_in[1].astype(F32)).astype(BF16)
    row_level[2] = row_in[0]
    row_level[4] = pair
    row_level[6] = row_in[2]
    row_level[7] = pair
    for place in range(1, NX):
        n = bin(place).count("1")

        @pl.when(across != place)
        def _():
            send(
                row_level.at[2 * place : 2 * place + n],
                row_level_in.at[pl.ds(2 * across, n)],
                send_sem.at[12],
                recv_sem.at[12],
                "seq",
                down * NX + place,
            )

        @pl.when(across == place)
        def _():
            row_level_in[2 * place : 2 * place + n] = row_level[2 * place : 2 * place + n]

    loads[6].wait()
    drain(cot.at[0 : toks - piece], recv_sem.at[1])
    for h in range(heads):
        cols = head_cols(h)
        near[:, cols] = weight[0, :, cols] * out[0, :, cols] + weight[1, :, cols] * out[1, :, cols]
        goal[:, cols] = cot[:, cols].astype(F32) * gain[:, cols]
        q_turned[h] = jnp.transpose(q[:, cols])
        for i in range(2):
            weighted[2 * h + i] = (
                scores[2 * h + i] * weight[0, span_rows(i), cols]
            ).astype(BF16)

    state[...] = jnp.zeros_like(state)
    for n in (1, 2):

        @pl.when(row_count == n)
        def _():
            drain(row_level_in.at[0 : (NX - 1) * n], recv_sem.at[12])

    slots = []
    for place in range(bits):
        if place in (0, 2):
            slot = jnp.int32(0)
        slots.append(slot)
        slot = slot + bit_of(me, place)
    for place in (0, 1):

        @pl.when(bit_of(me, place) == 1)
        def _():
            for h in range(heads):
                state[h, :, place * DH : (place + 1) * DH] = row_level_in[2 * h + slots[place]]

    for n in range(1, far_bits + 1):

        @pl.when(my_count == n)
        def _():
            drain(level_in.at[0 : (shards - 1) * n], recv_sem.at[2])

    for place in range(2, bits):

        @pl.when(bit_of(me, place) == 1)
        def _():
            for h in range(heads):
                for g in range(group):
                    state[h, g * rows : (g + 1) * rows, place * DH : (place + 1) * DH] = level_in[
                        (h * group + g) * far_bits + slots[place]
                    ]

    squares = jnp.zeros((toks, DH), F32)
    crosses = jnp.zeros((toks, DH), F32)
    for h in range(heads):
        cols = head_cols(h)
        far = mm(q[:, cols], state[h], NN)
        value = near[:, cols]
        for place in range(bits):
            part = far[:, place * DH : (place + 1) * DH]
            out[place + 2, :, cols] = part
            value = value + weight[place + 2, :, cols] * part
        value = value.astype(BF16)
        attn[:, cols] = value
        value = value.astype(F32)
        squares = squares + value * value
        crosses = crosses + goal[:, cols] * value
    one_row = jnp.ones((8, DH), BF16)
    for row, part in enumerate((squares, crosses)):
        high, low = split_two(part)
        both = mm(one_row, high, NT) + mm(one_row, low, NT)
        stat[row : row + 1, :] = both[0:1, :]

    def send_stat(peer):
        send(stat, stat_in.at[mine], send_sem.at[3], recv_sem.at[3], "head", peer)

    head_peers(send_stat)
    stat_in[mine] = stat[...]
    drain(stat_in.at[0 : members - 1], recv_sem.at[3])
    both = stat_in[0]
    for m in range(1, members):
        both = both + stat_in[m]
    inv_row = lax.rsqrt(both[0:1, :] * (1.0 / features) + EPSILON)
    mean_row = both[1:2, :] * inv_row * (1.0 / features)
    inv = jnp.transpose(jnp.broadcast_to(inv_row, (DH, toks)))
    mean = jnp.transpose(jnp.broadcast_to(mean_row, (DH, toks)))

    for h in range(heads):
        cols = head_cols(h)
        unit = attn[:, cols].astype(F32) * inv
        grad_h = ((goal[:, cols] - unit * mean) * inv).astype(BF16)
        grad[:, cols] = grad_h
        grad_f = grad_h.astype(F32)
        for place in range(bits):
            scaled[h, :, place * DH : (place + 1) * DH] = (
                weight[place + 2, :, cols] * grad_f
            ).astype(BF16)
        products = mm(q_turned[h], scaled[h], NN)
        for place in range(bits):

            @pl.when(bit_of(me, place) == 1)
            def _():
                part = products[:, place * DH : (place + 1) * DH].astype(BF16)
                if place < 2:
                    row_qg[2 * h + slots[place]] = part
                else:
                    for g in range(group):
                        qg[(h * group + g) * far_bits + slots[place]] = part[
                            g * rows : (g + 1) * rows
                        ]

    for n in range(1, far_bits + 1):

        @pl.when(my_count == n)
        def _():
            def send_qg(peer):
                send(
                    qg.at[pl.ds(peer * far_bits, n)],
                    qg_in.at[pl.ds(me * far_bits, n)],
                    send_sem.at[4],
                    recv_sem.at[4],
                    "seq",
                    peer,
                )

            seq_peers(send_qg)

    qg_in[pl.ds(me * far_bits, far_bits)] = qg[pl.ds(me * far_bits, far_bits)]
    for n in (1, 2):

        @pl.when(row_count == n)
        def _():
            def send_row_qg(place, peer):
                send(
                    row_qg.at[pl.ds(2 * place, n)],
                    row_qg_in.at[pl.ds(2 * across, n)],
                    send_sem.at[13],
                    recv_sem.at[13],
                    "seq",
                    peer,
                )

            row_peers(send_row_qg)
            row_qg_in[pl.ds(2 * across, n)] = row_qg[pl.ds(2 * across, n)]

    for h in range(heads):
        cols = head_cols(h)
        unit = attn[:, cols].astype(F32) * inv
        normed[:, cols] = (unit * gain[:, cols]).astype(BF16)
        gpart[:, cols] = jnp.sum(cot[:, cols].astype(F32) * unit, axis=0, keepdims=True)

    def send_gain(place, peer):
        send(gpart, gpart_in.at[across], send_sem.at[6], recv_sem.at[6], "seq", peer)

    row_peers(send_gain)
    gpart_in[across] = gpart[...]

    def send_normed(peer):
        send(
            normed.at[pl.ds(pl.multiple_of(peer * piece, piece), piece)],
            normed_out.at[:, my_cols],
            send_sem.at[5],
            recv_sem.at[5],
            "head",
            peer,
        )

    head_peers(send_normed)
    normed_out[:, my_cols] = normed[pl.ds(pl.multiple_of(mine * piece, piece), piece), :]

    lane_ids = lax.broadcasted_iota(jnp.int32, (8, width), 1) // DH
    head_rows = (
        (lax.broadcasted_iota(jnp.int32, (8, width), 0) == lane_ids).astype(F32).astype(BF16)
    )
    grad_all = grad[...].astype(F32)
    for l in range(levels):
        onehot = (idx[l : l + 1, :] == x_ids).astype(F32).astype(BF16)
        high, low = split_two(out[l] * grad_all)
        by_row = mm(onehot, high, NN) + mm(onehot, low, NN)
        high, low = split_two(by_row)
        result = mm(head_rows, high, NT) + mm(head_rows, low, NT)
        tpart[l] = result[0:heads, :]
    for l in range(levels):

        @pl.when(me != owner[l])
        def _():
            send(tpart.at[l], tpart_in.at[me], send_sem.at[7], recv_sem.at[7], "seq", owner[l])

        @pl.when(me == owner[l])
        def _():
            tpart_in[me] = tpart[l]

    for h in range(heads):
        cols = head_cols(h)
        grad_h = grad[:, cols]
        far = mm(scaled[h], state[h], NT)
        within = (weight[1, span_rows(1), cols] * grad_h[CH:].astype(F32)).astype(BF16)
        inner[h] = mm(q[span_rows(1), cols], within, TN)
        for i in range(2):
            at = (span_rows(i), cols)
            along = mm(grad_h[span_rows(i)], v[at], NT)
            first = weight[0, span_rows(i), cols]
            grad_scores = jnp.where(causal, along * first, 0.0).astype(BF16)
            value = far[span_rows(i)] + mm(grad_scores, k[at], NN)
            if i == 1:
                value = value + mm(within, intra[h], NT)
            dq[at] = value.astype(BF16)
            dk[at] = mm(grad_scores, q[at], TN)
            dv[at] = mm(weighted[2 * h + i], grad_h[span_rows(i)], TN)
        if h == 1:
            drain(gpart_in.at[0 : NX - 1], recv_sem.at[6])
            both = gpart_in[0]
            for c in range(1, NX):
                both = both + gpart_in[c]
            gline[...] = both
            gline_in[down] = both
            for offset in range(1, lines):
                line = lax.rem(down + offset, jnp.int32(lines))
                send(
                    gline,
                    gline_in.at[down],
                    send_sem.at[14],
                    recv_sem.at[14],
                    "seq",
                    line * NX + across,
                )


    for n in (0, 1, 2):

        @pl.when(row_count == n)
        def _():
            drain(row_qg_in.at[0 : NX - n], recv_sem.at[13])

    both = row_qg_in[4].astype(F32) + row_qg_in[7].astype(F32)
    row_ks[0] = (row_qg_in[2].astype(F32) + both).astype(BF16)
    row_ks[1] = both.astype(BF16)
    row_ks[2] = row_qg_in[6]
    row_ks[3] = jnp.zeros((DH, DH), BF16)
    row_ks_in[across] = row_ks[across]
    for place in range(NX - 1):

        @pl.when(across != place)
        def _():
            send(
                row_ks.at[place],
                row_ks_in.at[across],
                send_sem.at[15],
                recv_sem.at[15],
                "seq",
                down * NX + place,
            )

    @pl.when(across == NX - 1)
    def _():
        for place in range(NX - 1):
            row_ks_in[place] = jnp.zeros((DH, DH), BF16)

    for n in range(0, far_bits + 1):

        @pl.when(my_count == n)
        def _():
            drain(qg_in.at[0 : far_slots - n], recv_sem.at[4])

    def slot_of(line, place):
        return bin(line & ((1 << place) - 1)).count("1")

    reach = [None]
    for place in range(far_bits - 1, -1, -1):
        reach_next = []
        for block, above in enumerate(reach):
            upper = range((2 * block + 1) << place, (2 * block + 2) << place)
            part = functools.reduce(
                lambda a, b: a + b,
                [
                    qg_in[c * far_bits + slot_of(line, place)].astype(F32)
                    for line in upper
                    for c in range(NX * line, NX * line + NX)
                ],
            )
            reach_next.append(part if above is None else above + part)
            reach_next.append(above)
        reach = reach_next
    for line in range(lines):
        block = jnp.zeros((rows, DH), BF16) if reach[line] is None else reach[line].astype(BF16)
        for c in range(NX * line, NX * line + NX):
            ks[c] = block

    def send_ks(peer):
        send(ks.at[peer], ks_in.at[me], send_sem.at[9], recv_sem.at[9], "seq", peer)

    seq_peers(send_ks)
    ks_in[me] = ks[me]

    if lines > 1:
        drain(gline_in.at[0 : lines - 1], recv_sem.at[14])
    both = gline_in[0]
    for c in range(1, lines):
        both = both + gline_in[c]
    gsum[...] = both

    def send_gsum(peer):
        send(gsum, gall.at[:, my_cols], send_sem.at[8], recv_sem.at[8], "head", peer)

    head_peers(send_gsum)
    gall[:, my_cols] = both

    for l in range(levels):

        @pl.when(me == owner[l])
        def _():
            drain(tpart_in.at[0 : shards - 1], recv_sem.at[7])
            both = tpart_in[0]
            for c in range(1, shards):
                both = both + tpart_in[c]
            tsum[l] = both

            def send_tsum(peer):
                send(tsum.at[l], tsum.at[l], send_sem.at[10], tab_sem.at[l], "seq", peer)

            seq_peers(send_tsum)

    drain(ks_in.at[0 : shards - 1], recv_sem.at[9])

    @pl.when(across != NX - 1)
    def _():
        drain(row_ks_in.at[0 : NX - 1], recv_sem.at[15])

    for h in range(heads):
        cols = head_cols(h)
        cross = ks_in[h * group : (h + 1) * group].reshape(DH, DH).astype(F32)
        cross = cross + row_ks_in[h].astype(F32)
        for i in range(2):
            at = (span_rows(i), cols)
            key_state = (cross + inner[h] if i == 0 else cross).astype(BF16)
            dk_bf[at] = (dk[at] + mm(v[at], key_state, NT)).astype(BF16)
            dv_bf[at] = (dv[at] + mm(k[at], key_state, NN)).astype(BF16)

    drain(gall.at[:, 0 : features - width], recv_sem.at[8])
    for l in range(levels):

        @pl.when(me != owner[l])
        def _():
            drain(tsum.at[l], tab_sem.at[l])

    drain(normed_out.at[:, 0 : features - width], recv_sem.at[5])
    drain(total.at[0 : (shards - 1) * rows], send_sem.at[0])
    drain(cot.at[0 : toks - piece], send_sem.at[1])
    drain(stat_in.at[0 : members - 1], send_sem.at[3])
    for n in range(0, far_bits + 1):

        @pl.when(my_count == n)
        def _():
            drain(level.at[0 : far_slots - n], send_sem.at[2])
            if n:
                drain(qg.at[0 : (shards - 1) * n], send_sem.at[4])

    drain(row_in.at[0 : NX - 1], send_sem.at[11])
    for n in (0, 1, 2):

        @pl.when(row_count == n)
        def _():
            drain(row_level.at[0 : NX - n], send_sem.at[12])
            if n:
                drain(row_qg.at[0 : (NX - 1) * n], send_sem.at[13])

    @pl.when(across == NX - 1)
    def _():
        drain(row_ks.at[0 : NX - 1], send_sem.at[15])

    @pl.when(across != NX - 1)
    def _():
        drain(row_ks.at[0 : NX - 2], send_sem.at[15])

    if lines > 1:
        drain(gline_in.at[0 : lines - 1], send_sem.at[14])
    drain(normed.at[0 : toks - piece], send_sem.at[5])
    drain(gpart_in.at[0 : NX - 1], send_sem.at[6])
    drain(gall.at[:, 0 : features - width], send_sem.at[8])
    drain(ks_in.at[0 : shards - 1], send_sem.at[9])

    is_owner = functools.reduce(lambda a, b: a | b, [me == owner[l] for l in range(levels)])

    @pl.when(is_owner)
    def _():
        drain(tpart.at[0 : levels - 1], send_sem.at[7])
        drain(tpart_in.at[0 : shards - 1], send_sem.at[10])

    @pl.when(jnp.logical_not(is_owner))
    def _():
        drain(tpart, send_sem.at[7])


def copy_kernel(*refs):
    count = len(refs) // 2
    sems = refs[-1]
    copies = [
        pltpu.make_async_copy(refs[i], refs[count + i], sems.at[i]) for i in range(count)
    ]
    for copy in copies:
        copy.start()
    for copy in copies:
        copy.wait()


def body(shards, members, queries, key_rows, value_rows, level_table, level_index, norm_gain, cotangent):
    toks, width = queries.shape
    table, levels, heads = level_table.shape
    features = norm_gain.shape[0]
    bits = shards.bit_length() - 1
    rows = heads * DH // shards
    anywhere = pl.BlockSpec(memory_space=pl.ANY)
    vmem = pltpu.VMEM
    outs = pl.pallas_call(
        functools.partial(kernel, shards, members),
        out_shape=(
            jax.ShapeDtypeStruct(cotangent.shape, BF16),
            jax.ShapeDtypeStruct((toks, width), BF16),
            jax.ShapeDtypeStruct((toks, width), BF16),
            jax.ShapeDtypeStruct((toks, width), BF16),
            jax.ShapeDtypeStruct((levels, heads, table), F32),
            jax.ShapeDtypeStruct((1, features), F32),
        ),
        in_specs=[anywhere] * 7,
        out_specs=[pl.BlockSpec(memory_space=pltpu.VMEM)] * 6,
        scratch_shapes=[
            vmem((toks, width), BF16),
            vmem((toks, width), BF16),
            vmem((toks, width), BF16),
            vmem((levels, heads, table), F32),
            vmem((levels, toks), jnp.int32),
            vmem((1, width), F32),
            vmem((toks, width), BF16),
            vmem((heads * DH, DH), BF16),
            vmem((shards, rows, DH), BF16),
            vmem((shards * (bits - 2), rows, DH), BF16),
            vmem((shards * (bits - 2), rows, DH), BF16),
            vmem((heads, DH, bits * DH), BF16),
            vmem((heads, DH, DH), BF16),
            vmem((levels, toks, width), F32),
            vmem((levels, toks, width), F32),
            vmem((2 * heads, CH, CH), F32),
            vmem((toks, width), BF16),
            vmem((2, toks), F32),
            vmem((members, 2, toks), F32),
            vmem((toks, width), BF16),
            vmem((1, width), F32),
            vmem((NX, 1, width), F32),
            vmem((1, width), F32),
            vmem((toks, width), BF16),
            vmem((shards * (bits - 2), rows, DH), BF16),
            vmem((shards * (bits - 2), rows, DH), BF16),
            vmem((heads, DH, DH), F32),
            vmem((shards, rows, DH), BF16),
            vmem((shards, rows, DH), BF16),
            vmem((toks, width), F32),
            vmem((toks, width), F32),
            vmem((levels, heads, table), F32),
            vmem((shards, heads, table), F32),
            vmem((toks, width), F32),
            vmem((toks, width), F32),
            vmem((2 * heads, CH, CH), BF16),
            vmem((heads, toks, bits * DH), BF16),
            vmem((NX, DH, DH), BF16),
            vmem((2 * NX, DH, DH), BF16),
            vmem((2 * NX, DH, DH), BF16),
            vmem((2 * NX, DH, DH), BF16),
            vmem((2 * NX, DH, DH), BF16),
            vmem((NX, DH, DH), BF16),
            vmem((NX, DH, DH), BF16),
            vmem((1, width), F32),
            vmem((shards // NX, 1, width), F32),
            vmem((heads, DH, toks), BF16),
            pltpu.SemaphoreType.DMA((7,)),
            pltpu.SemaphoreType.DMA((16,)),
            pltpu.SemaphoreType.DMA((16,)),
            pltpu.SemaphoreType.DMA((levels,)),
        ],
        compiler_params=pltpu.CompilerParams(
            collective_id=0, has_side_effects=True, vmem_limit_bytes=VMEM_BYTES
        ),
    )(
        *(
            pltpu.with_memory_space_constraint(array, pltpu.HBM)
            for array in (
                queries,
                key_rows,
                value_rows,
                jnp.transpose(level_table, (1, 2, 0)),
                jnp.transpose(level_index),
                norm_gain.reshape(1, features),
                cotangent,
            )
        )
    )
    normed, dq, dk, dv, gtab, ggain = pl.pallas_call(
        copy_kernel,
        out_shape=tuple(jax.ShapeDtypeStruct(o.shape, o.dtype) for o in outs),
        in_specs=[pl.BlockSpec(memory_space=pltpu.VMEM)] * 6,
        out_specs=[anywhere] * 6,
        scratch_shapes=[pltpu.SemaphoreType.DMA((6,))],
        compiler_params=pltpu.CompilerParams(vmem_limit_bytes=4 * 2**20),
    )(*outs)
    return normed, dq, dk, dv, jnp.transpose(gtab, (2, 0, 1)), ggain.reshape(features)


def solution(mesh):
    wide = P("seq", "head")
    rows = P(("seq", "head"), None)
    table = P(None, None, "head")
    return jax.shard_map(
        functools.partial(body, mesh.shape["seq"], mesh.shape["head"]),
        mesh=mesh,
        in_specs=(wide, wide, wide, table, P("seq", None), P(), rows),
        out_specs=(rows, wide, wide, wide, table, P()),
        check_vma=False,
    )
```

```python
import functools

import jax
import jax.numpy as jnp
from jax import lax
from jax.experimental import pallas as pl
from jax.experimental.pallas import tpu as pltpu
from jax.sharding import PartitionSpec as P

CH = 128
DH = 128
EPSILON = 1e-06
NX = 4
VMEM_BYTES = 48 * 2**20
MESH = pl.DeviceIdType.MESH
F32 = jnp.float32
BF16 = jnp.bfloat16

NN = (((1,), (0,)), ((), ()))
NT = (((1,), (1,)), ((), ()))
TN = (((0,), (0,)), ((), ()))


def mm(a, b, dims):
    return lax.dot_general(a, b, dims, preferred_element_type=F32)


def split_two(value):
    high = value.astype(BF16)
    low = (value - high.astype(F32)).astype(BF16)
    return high, low


def bit_of(index, place):
    return lax.rem(lax.div(index, jnp.int32(2**place)), jnp.int32(2))


def send(src, dst, send_sem, recv_sem, axis, target):
    pltpu.make_async_remote_copy(
        src_ref=src,
        dst_ref=dst,
        send_sem=send_sem,
        recv_sem=recv_sem,
        device_id={axis: target},
        device_id_type=MESH,
    ).start()


def drain(view, sem):
    pltpu.make_async_copy(view, view, sem).wait()


def kernel(
    shards,
    members,
    q_in,
    k_in,
    v_in,
    tab_in,
    idx_in,
    gain_in,
    cot_in,
    normed_out,
    dq,
    dk_bf,
    dv_bf,
    tsum,
    gall,
    q,
    k,
    v,
    tab,
    idx,
    gain,
    cot,
    total,
    total_in,
    level,
    level_in,
    state,
    intra,
    weight,
    out,
    scores,
    attn,
    stat,
    stat_in,
    normed,
    gpart,
    gpart_in,
    gsum,
    grad,
    qg,
    qg_in,
    inner,
    ks,
    ks_in,
    dk,
    dv,
    tpart,
    tpart_in,
    near,
    goal,
    weighted,
    scaled,
    row_in,
    row_level,
    row_level_in,
    row_qg,
    row_qg_in,
    row_ks,
    row_ks_in,
    gline,
    gline_in,
    q_turned,
    load_sem,
    send_sem,
    recv_sem,
    tab_sem,
):
    me = lax.axis_index("seq")
    mine = lax.axis_index("head")
    bits = shards.bit_length() - 1
    far_bits = bits - 2
    lines = shards // NX
    toks, width = q.shape
    heads = width // DH
    levels = bits + 2
    rows = heads * DH // shards
    group = shards // heads
    piece = toks // members
    table = tab.shape[2]
    features = members * width

    def head_cols(h):
        return slice(h * DH, (h + 1) * DH)

    def span_rows(i):
        return slice(i * CH, (i + 1) * CH)

    def from_far(index, count):
        step = lax.rem(index, jnp.int32(2))
        return count // 2 + (1 - 2 * step) * lax.div(index + 1, jnp.int32(2))

    def seq_peers(step):
        def one(index, carry):
            line = lax.div(me, jnp.int32(NX)) + from_far(lax.div(index, jnp.int32(NX)), lines)
            place = lax.rem(me, jnp.int32(NX)) + from_far(lax.rem(index, jnp.int32(NX)), NX)
            step(lax.rem(line, jnp.int32(lines)) * NX + lax.rem(place, jnp.int32(NX)))
            return carry

        lax.fori_loop(0, shards - 1, one, 0)

    def head_peers(step):
        def one(index, carry):
            along = lax.div(mine, jnp.int32(2)) + from_far(lax.div(index, jnp.int32(2)), members // 2)
            core = lax.rem(mine, jnp.int32(2)) + from_far(lax.rem(index, jnp.int32(2)), 2)
            step(lax.rem(along, jnp.int32(members // 2)) * 2 + lax.rem(core, jnp.int32(2)))
            return carry

        lax.fori_loop(0, members - 1, one, 0)

    def ones_in(index):
        count = jnp.int32(0)
        for place in range(2, bits):
            count = count + bit_of(index, place)
        return count

    my_count = ones_in(me)
    across = lax.rem(me, jnp.int32(NX))
    down = lax.div(me, jnp.int32(NX))
    row_count = bit_of(me, 0) + bit_of(me, 1)
    far_slots = far_bits * shards // 2
    owner = [(NX + 1) * l % shards for l in range(levels)]

    def row_peers(step):
        for offset in range(1, NX):
            place = lax.rem(across + offset, jnp.int32(NX))
            step(place, down * NX + place)

    my_cols = pl.ds(pl.multiple_of(mine * width, width), width)

    loads = [
        pltpu.make_async_copy(k_in, k, load_sem.at[0]),
        pltpu.make_async_copy(v_in, v, load_sem.at[1]),
        pltpu.make_async_copy(q_in, q, load_sem.at[2]),
        pltpu.make_async_copy(tab_in, tab, load_sem.at[3]),
        pltpu.make_async_copy(idx_in, idx, load_sem.at[4]),
        pltpu.make_async_copy(gain_in.at[:, my_cols], gain, load_sem.at[5]),
        pltpu.make_async_copy(
            cot_in.at[:, my_cols],
            cot.at[pl.ds(pl.multiple_of(mine * piece, piece), piece)],
            load_sem.at[6],
        ),
    ]
    for copy in loads:
        copy.start()

    barrier = pltpu.get_barrier_semaphore()

    def greet_seq(offset, carry):
        peer = lax.rem(me + offset, jnp.int32(shards))
        pl.semaphore_signal(barrier, inc=1, device_id={"seq": peer}, device_id_type=MESH)
        return carry

    def greet_head(offset, carry):
        peer = lax.rem(mine + offset, jnp.int32(members))
        pl.semaphore_signal(barrier, inc=1, device_id={"head": peer}, device_id_type=MESH)
        return carry

    lax.fori_loop(1, shards, greet_seq, 0)
    lax.fori_loop(1, members, greet_head, 0)

    loads[0].wait()
    loads[1].wait()
    for h in range(heads):
        first = mm(k[span_rows(0), head_cols(h)], v[span_rows(0), head_cols(h)], TN)
        second = mm(k[span_rows(1), head_cols(h)], v[span_rows(1), head_cols(h)], TN)
        intra[h] = first.astype(BF16)
        total[h * DH : (h + 1) * DH, :] = (first + second).astype(BF16)

    pl.semaphore_wait(barrier, shards + members - 2)

    def send_total(peer):
        send(
            total.at[pl.ds(pl.multiple_of(peer * rows, rows), rows)],
            total_in.at[me],
            send_sem.at[0],
            recv_sem.at[0],
            "seq",
            peer,
        )

    @pl.when(down != lines - 1)
    def _():
        seq_peers(send_total)


    def send_row(place, peer):
        send(
            total.at[pl.ds(pl.multiple_of(place * DH, DH), DH)],
            row_in.at[across],
            send_sem.at[11],
            recv_sem.at[11],
            "seq",
            peer,
        )

    row_peers(send_row)

    def send_cot(peer):
        send(
            cot_in.at[:, pl.ds(pl.multiple_of(peer * width, width), width)],
            cot.at[pl.ds(pl.multiple_of(mine * piece, piece), piece)],
            send_sem.at[1],
            recv_sem.at[1],
            "head",
            peer,
        )

    head_peers(send_cot)
    total_in[me] = total[pl.ds(pl.multiple_of(me * rows, rows), rows), :]
    row_in[across] = total[pl.ds(pl.multiple_of(across * DH, DH), DH), :]

    for copy in loads[2:6]:
        copy.wait()
    x_ids = lax.broadcasted_iota(jnp.int32, (table, toks), 0)
    stacked = []
    for l in range(levels):
        onehot = (idx[l : l + 1, :] == x_ids).astype(F32).astype(BF16)
        high, low = split_two(tab[l])
        stacked.append(mm(high, onehot, NN))
        stacked.append(mm(low, onehot, NN))
    pad = 128 - 2 * heads * levels
    stacked.append(jnp.zeros((pad, toks), F32))
    columns = jnp.transpose(jnp.concatenate(stacked, axis=0)).astype(BF16)
    row_ids = lax.broadcasted_iota(jnp.int32, (128, width), 0)
    col_head = lax.broadcasted_iota(jnp.int32, (128, width), 1) // DH
    for l in range(levels):
        base = 2 * heads * l
        pick = (row_ids == base + col_head) | (row_ids == base + heads + col_head)
        weight[l] = mm(columns, pick.astype(F32).astype(BF16), NN)

    causal = lax.broadcasted_iota(jnp.int32, (CH, CH), 1) <= lax.broadcasted_iota(
        jnp.int32, (CH, CH), 0
    )
    for h in range(heads):
        for i in range(2):
            at = (span_rows(i), head_cols(h))
            score = jnp.where(causal, mm(q[at], k[at], NT), 0.0)
            scores[2 * h + i] = score
            out[0, at[0], at[1]] = mm(score.astype(BF16), v[at], NN)
        out[1, span_rows(0), head_cols(h)] = jnp.zeros((CH, DH), F32)
        out[1, span_rows(1), head_cols(h)] = mm(
            q[span_rows(1), head_cols(h)], intra[h], NN
        )

    @pl.when(down != lines - 1)
    def _():
        drain(total_in.at[0 : shards - NX - 1], recv_sem.at[0])

    @pl.when(down == lines - 1)
    def _():
        drain(total_in.at[0 : shards - NX], recv_sem.at[0])

    sums = [
        functools.reduce(
            lambda a, b: a + b,
            [total_in[NX * line + place].astype(F32) for place in range(NX)],
        )
        for line in range(lines)
    ]
    sums = [sums]
    for place in range(1, far_bits):
        below = sums[-1]
        sums.append([below[2 * j] + below[2 * j + 1] for j in range(len(below) // 2)])
    for line in range(lines):
        slot = 0
        for place in range(far_bits):
            if (line >> place) & 1:
                block = sums[place][(line >> place) ^ 1].astype(BF16)
                for c in range(NX * line, NX * line + NX):
                    level[c * far_bits + slot] = block
                slot += 1

    def send_line(index, places):
        line = lax.rem(down + from_far(index, lines), jnp.int32(lines))
        count = ones_in(line * NX)
        for n in range(1, far_bits + 1):

            @pl.when(count == n)
            def _():
                for i in range(places):
                    step = 2 - (i + 1) // 2 if i % 2 else 2 + i // 2
                    peer = line * NX + lax.rem(across + step, jnp.int32(NX))
                    send(
                        level.at[pl.ds(peer * far_bits, n)],
                        level_in.at[pl.ds(me * far_bits, n)],
                        send_sem.at[2],
                        recv_sem.at[2],
                        "seq",
                        peer,
                    )

    def whole_line(index, carry):
        send_line(index, NX)
        return carry

    lax.fori_loop(0, lines - 1, whole_line, 0)
    send_line(jnp.int32(lines - 1), NX - 1)
    level_in[pl.ds(me * far_bits, far_bits)] = level[pl.ds(me * far_bits, far_bits)]

    drain(row_in.at[0 : NX - 1], recv_sem.at[11])
    pair = (row_in[0].astype(F32) + row_in[1].astype(F32)).astype(BF16)
    row_level[2] = row_in[0]
    row_level[4] = pair
    row_level[6] = row_in[2]
    row_level[7] = pair
    for place in range(1, NX):
        n = bin(place).count("1")

        @pl.when(across != place)
        def _():
            send(
                row_level.at[2 * place : 2 * place + n],
                row_level_in.at[pl.ds(2 * across, n)],
                send_sem.at[12],
                recv_sem.at[12],
                "seq",
                down * NX + place,
            )

        @pl.when(across == place)
        def _():
            row_level_in[2 * place : 2 * place + n] = row_level[2 * place : 2 * place + n]

    loads[6].wait()
    drain(cot.at[0 : toks - piece], recv_sem.at[1])
    for h in range(heads):
        cols = head_cols(h)
        near[:, cols] = weight[0, :, cols] * out[0, :, cols] + weight[1, :, cols] * out[1, :, cols]
        goal[:, cols] = cot[:, cols].astype(F32) * gain[:, cols]
        q_turned[h] = jnp.transpose(q[:, cols])
        for i in range(2):
            weighted[2 * h + i] = (
                scores[2 * h + i] * weight[0, span_rows(i), cols]
            ).astype(BF16)

    state[...] = jnp.zeros_like(state)
    for n in (1, 2):

        @pl.when(row_count == n)
        def _():
            drain(row_level_in.at[0 : (NX - 1) * n], recv_sem.at[12])

    slots = []
    for place in range(bits):
        if place in (0, 2):
            slot = jnp.int32(0)
        slots.append(slot)
        slot = slot + bit_of(me, place)
    for place in (0, 1):

        @pl.when(bit_of(me, place) == 1)
        def _():
            for h in range(heads):
                state[h, :, place * DH : (place + 1) * DH] = row_level_in[2 * h + slots[place]]

    for n in range(1, far_bits + 1):

        @pl.when(my_count == n)
        def _():
            drain(level_in.at[0 : (shards - 1) * n], recv_sem.at[2])

    for place in range(2, bits):

        @pl.when(bit_of(me, place) == 1)
        def _():
            for h in range(heads):
                for g in range(group):
                    state[h, g * rows : (g + 1) * rows, place * DH : (place + 1) * DH] = level_in[
                        (h * group + g) * far_bits + slots[place]
                    ]

    squares = jnp.zeros((toks, DH), F32)
    crosses = jnp.zeros((toks, DH), F32)
    for h in range(heads):
        cols = head_cols(h)
        far = mm(q[:, cols], state[h], NN)
        value = near[:, cols]
        for place in range(bits):
            part = far[:, place * DH : (place + 1) * DH]
            out[place + 2, :, cols] = part
            value = value + weight[place + 2, :, cols] * part
        value = value.astype(BF16)
        attn[:, cols] = value
        value = value.astype(F32)
        squares = squares + value * value
        crosses = crosses + goal[:, cols] * value
    one_row = jnp.ones((8, DH), BF16)
    for row, part in enumerate((squares, crosses)):
        high, low = split_two(part)
        both = mm(one_row, high, NT) + mm(one_row, low, NT)
        stat[row : row + 1, :] = both[0:1, :]

    def send_stat(peer):
        send(stat, stat_in.at[mine], send_sem.at[3], recv_sem.at[3], "head", peer)

    head_peers(send_stat)
    stat_in[mine] = stat[...]
    drain(stat_in.at[0 : members - 1], recv_sem.at[3])
    both = stat_in[0]
    for m in range(1, members):
        both = both + stat_in[m]
    inv_row = lax.rsqrt(both[0:1, :] * (1.0 / features) + EPSILON)
    mean_row = both[1:2, :] * inv_row * (1.0 / features)
    inv = jnp.transpose(jnp.broadcast_to(inv_row, (DH, toks)))
    mean = jnp.transpose(jnp.broadcast_to(mean_row, (DH, toks)))

    for h in range(heads):
        cols = head_cols(h)
        unit = attn[:, cols].astype(F32) * inv
        grad_h = ((goal[:, cols] - unit * mean) * inv).astype(BF16)
        grad[:, cols] = grad_h
        grad_f = grad_h.astype(F32)
        for place in range(bits):
            scaled[h, :, place * DH : (place + 1) * DH] = (
                weight[place + 2, :, cols] * grad_f
            ).astype(BF16)
        products = mm(q_turned[h], scaled[h], NN)
        for place in range(bits):

            @pl.when(bit_of(me, place) == 1)
            def _():
                part = products[:, place * DH : (place + 1) * DH].astype(BF16)
                if place < 2:
                    row_qg[2 * h + slots[place]] = part
                else:
                    for g in range(group):
                        qg[(h * group + g) * far_bits + slots[place]] = part[
                            g * rows : (g + 1) * rows
                        ]

    for n in range(1, far_bits + 1):

        @pl.when(my_count == n)
        def _():
            def send_qg(peer):
                send(
                    qg.at[pl.ds(peer * far_bits, n)],
                    qg_in.at[pl.ds(me * far_bits, n)],
                    send_sem.at[4],
                    recv_sem.at[4],
                    "seq",
                    peer,
                )

            seq_peers(send_qg)

    qg_in[pl.ds(me * far_bits, far_bits)] = qg[pl.ds(me * far_bits, far_bits)]
    for n in (1, 2):

        @pl.when(row_count == n)
        def _():
            def send_row_qg(place, peer):
                send(
                    row_qg.at[pl.ds(2 * place, n)],
                    row_qg_in.at[pl.ds(2 * across, n)],
                    send_sem.at[13],
                    recv_sem.at[13],
                    "seq",
                    peer,
                )

            row_peers(send_row_qg)
            row_qg_in[pl.ds(2 * across, n)] = row_qg[pl.ds(2 * across, n)]

    for h in range(heads):
        cols = head_cols(h)
        unit = attn[:, cols].astype(F32) * inv
        normed[:, cols] = (unit * gain[:, cols]).astype(BF16)
        gpart[:, cols] = jnp.sum(cot[:, cols].astype(F32) * unit, axis=0, keepdims=True)

    def send_gain(place, peer):
        send(gpart, gpart_in.at[across], send_sem.at[6], recv_sem.at[6], "seq", peer)

    row_peers(send_gain)
    gpart_in[across] = gpart[...]

    def send_normed(peer):
        send(
            normed.at[pl.ds(pl.multiple_of(peer * piece, piece), piece)],
            normed_out.at[:, my_cols],
            send_sem.at[5],
            recv_sem.at[5],
            "head",
            peer,
        )

    head_peers(send_normed)
    normed_out[:, my_cols] = normed[pl.ds(pl.multiple_of(mine * piece, piece), piece), :]

    lane_ids = lax.broadcasted_iota(jnp.int32, (8, width), 1) // DH
    head_rows = (
        (lax.broadcasted_iota(jnp.int32, (8, width), 0) == lane_ids).astype(F32).astype(BF16)
    )
    grad_all = grad[...].astype(F32)
    for l in range(levels):
        onehot = (idx[l : l + 1, :] == x_ids).astype(F32).astype(BF16)
        high, low = split_two(out[l] * grad_all)
        by_row = mm(onehot, high, NN) + mm(onehot, low, NN)
        high, low = split_two(by_row)
        result = mm(head_rows, high, NT) + mm(head_rows, low, NT)
        tpart[l] = result[0:heads, :]
    for l in range(levels):

        @pl.when(me != owner[l])
        def _():
            send(tpart.at[l], tpart_in.at[me], send_sem.at[7], recv_sem.at[7], "seq", owner[l])

        @pl.when(me == owner[l])
        def _():
            tpart_in[me] = tpart[l]

    for h in range(heads):
        cols = head_cols(h)
        grad_h = grad[:, cols]
        far = mm(scaled[h], state[h], NT)
        within = (weight[1, span_rows(1), cols] * grad_h[CH:].astype(F32)).astype(BF16)
        inner[h] = mm(q[span_rows(1), cols], within, TN)
        for i in range(2):
            at = (span_rows(i), cols)
            along = mm(grad_h[span_rows(i)], v[at], NT)
            first = weight[0, span_rows(i), cols]
            grad_scores = jnp.where(causal, along * first, 0.0).astype(BF16)
            value = far[span_rows(i)] + mm(grad_scores, k[at], NN)
            if i == 1:
                value = value + mm(within, intra[h], NT)
            dq[at] = value.astype(BF16)
            dk[at] = mm(grad_scores, q[at], TN)
            dv[at] = mm(weighted[2 * h + i], grad_h[span_rows(i)], TN)
        if h == 1:
            drain(gpart_in.at[0 : NX - 1], recv_sem.at[6])
            both = gpart_in[0]
            for c in range(1, NX):
                both = both + gpart_in[c]
            gline[...] = both
            gline_in[down] = both
            for offset in range(1, lines):
                line = lax.rem(down + offset, jnp.int32(lines))
                send(
                    gline,
                    gline_in.at[down],
                    send_sem.at[14],
                    recv_sem.at[14],
                    "seq",
                    line * NX + across,
                )


    for n in (0, 1, 2):

        @pl.when(row_count == n)
        def _():
            drain(row_qg_in.at[0 : NX - n], recv_sem.at[13])

    both = row_qg_in[4].astype(F32) + row_qg_in[7].astype(F32)
    row_ks[0] = (row_qg_in[2].astype(F32) + both).astype(BF16)
    row_ks[1] = both.astype(BF16)
    row_ks[2] = row_qg_in[6]
    row_ks[3] = jnp.zeros((DH, DH), BF16)
    row_ks_in[across] = row_ks[across]
    for place in range(NX - 1):

        @pl.when(across != place)
        def _():
            send(
                row_ks.at[place],
                row_ks_in.at[across],
                send_sem.at[15],
                recv_sem.at[15],
                "seq",
                down * NX + place,
            )

    @pl.when(across == NX - 1)
    def _():
        for place in range(NX - 1):
            row_ks_in[place] = jnp.zeros((DH, DH), BF16)

    for n in range(0, far_bits + 1):

        @pl.when(my_count == n)
        def _():
            drain(qg_in.at[0 : far_slots - n], recv_sem.at[4])

    def slot_of(line, place):
        return bin(line & ((1 << place) - 1)).count("1")

    reach = [None]
    for place in range(far_bits - 1, -1, -1):
        reach_next = []
        for block, above in enumerate(reach):
            upper = range((2 * block + 1) << place, (2 * block + 2) << place)
            part = functools.reduce(
                lambda a, b: a + b,
                [
                    qg_in[c * far_bits + slot_of(line, place)].astype(F32)
                    for line in upper
                    for c in range(NX * line, NX * line + NX)
                ],
            )
            reach_next.append(part if above is None else above + part)
            reach_next.append(above)
        reach = reach_next
    for line in range(lines):
        block = jnp.zeros((rows, DH), BF16) if reach[line] is None else reach[line].astype(BF16)
        for c in range(NX * line, NX * line + NX):
            ks[c] = block

    def send_ks(peer):
        @pl.when(lax.div(peer, jnp.int32(NX)) != lines - 1)
        def _():
            send(ks.at[peer], ks_in.at[me], send_sem.at[9], recv_sem.at[9], "seq", peer)

    seq_peers(send_ks)
    @pl.when(down != lines - 1)
    def _():
        ks_in[me] = ks[me]

    @pl.when(down == lines - 1)
    def _():
        ks_in[...] = jnp.zeros_like(ks_in)

    if lines > 1:
        drain(gline_in.at[0 : lines - 1], recv_sem.at[14])
    both = gline_in[0]
    for c in range(1, lines):
        both = both + gline_in[c]
    gsum[...] = both

    def send_gsum(peer):
        send(gsum, gall.at[:, my_cols], send_sem.at[8], recv_sem.at[8], "head", peer)

    head_peers(send_gsum)
    gall[:, my_cols] = both

    for l in range(levels):

        @pl.when(me == owner[l])
        def _():
            drain(tpart_in.at[0 : shards - 1], recv_sem.at[7])
            both = tpart_in[0]
            for c in range(1, shards):
                both = both + tpart_in[c]
            tsum[l] = both

            def send_tsum(peer):
                send(tsum.at[l], tsum.at[l], send_sem.at[10], tab_sem.at[l], "seq", peer)

            seq_peers(send_tsum)

    @pl.when(down != lines - 1)
    def _():
        drain(ks_in.at[0 : shards - 1], recv_sem.at[9])

    @pl.when(across != NX - 1)
    def _():
        drain(row_ks_in.at[0 : NX - 1], recv_sem.at[15])

    for h in range(heads):
        cols = head_cols(h)
        cross = ks_in[h * group : (h + 1) * group].reshape(DH, DH).astype(F32)
        cross = cross + row_ks_in[h].astype(F32)
        for i in range(2):
            at = (span_rows(i), cols)
            key_state = (cross + inner[h] if i == 0 else cross).astype(BF16)
            dk_bf[at] = (dk[at] + mm(v[at], key_state, NT)).astype(BF16)
            dv_bf[at] = (dv[at] + mm(k[at], key_state, NN)).astype(BF16)

    drain(gall.at[:, 0 : features - width], recv_sem.at[8])
    for l in range(levels):

        @pl.when(me != owner[l])
        def _():
            drain(tsum.at[l], tab_sem.at[l])

    drain(normed_out.at[:, 0 : features - width], recv_sem.at[5])
    @pl.when(down != lines - 1)
    def _():
        drain(total.at[0 : (shards - 1) * rows], send_sem.at[0])

    drain(cot.at[0 : toks - piece], send_sem.at[1])
    drain(stat_in.at[0 : members - 1], send_sem.at[3])
    for n in range(0, far_bits + 1):

        @pl.when(my_count == n)
        def _():
            drain(level.at[0 : far_slots - n], send_sem.at[2])
            if n:
                drain(qg.at[0 : (shards - 1) * n], send_sem.at[4])

    drain(row_in.at[0 : NX - 1], send_sem.at[11])
    for n in (0, 1, 2):

        @pl.when(row_count == n)
        def _():
            drain(row_level.at[0 : NX - n], send_sem.at[12])
            if n:
                drain(row_qg.at[0 : (NX - 1) * n], send_sem.at[13])

    @pl.when(across == NX - 1)
    def _():
        drain(row_ks.at[0 : NX - 1], send_sem.at[15])

    @pl.when(across != NX - 1)
    def _():
        drain(row_ks.at[0 : NX - 2], send_sem.at[15])

    if lines > 1:
        drain(gline_in.at[0 : lines - 1], send_sem.at[14])
    drain(normed.at[0 : toks - piece], send_sem.at[5])
    drain(gpart_in.at[0 : NX - 1], send_sem.at[6])
    drain(gall.at[:, 0 : features - width], send_sem.at[8])
    @pl.when(down != lines - 1)
    def _():
        drain(ks_in.at[0 : shards - NX - 1], send_sem.at[9])

    @pl.when(down == lines - 1)
    def _():
        drain(ks_in.at[0 : shards - NX], send_sem.at[9])

    is_owner = functools.reduce(lambda a, b: a | b, [me == owner[l] for l in range(levels)])

    @pl.when(is_owner)
    def _():
        drain(tpart.at[0 : levels - 1], send_sem.at[7])
        drain(tpart_in.at[0 : shards - 1], send_sem.at[10])

    @pl.when(jnp.logical_not(is_owner))
    def _():
        drain(tpart, send_sem.at[7])


def copy_kernel(*refs):
    count = len(refs) // 2
    sems = refs[-1]
    copies = [
        pltpu.make_async_copy(refs[i], refs[count + i], sems.at[i]) for i in range(count)
    ]
    for copy in copies:
        copy.start()
    for copy in copies:
        copy.wait()


def body(shards, members, queries, key_rows, value_rows, level_table, level_index, norm_gain, cotangent):
    toks, width = queries.shape
    table, levels, heads = level_table.shape
    features = norm_gain.shape[0]
    bits = shards.bit_length() - 1
    rows = heads * DH // shards
    anywhere = pl.BlockSpec(memory_space=pl.ANY)
    vmem = pltpu.VMEM
    outs = pl.pallas_call(
        functools.partial(kernel, shards, members),
        out_shape=(
            jax.ShapeDtypeStruct(cotangent.shape, BF16),
            jax.ShapeDtypeStruct((toks, width), BF16),
            jax.ShapeDtypeStruct((toks, width), BF16),
            jax.ShapeDtypeStruct((toks, width), BF16),
            jax.ShapeDtypeStruct((levels, heads, table), F32),
            jax.ShapeDtypeStruct((1, features), F32),
        ),
        in_specs=[anywhere] * 7,
        out_specs=[pl.BlockSpec(memory_space=pltpu.VMEM)] * 6,
        scratch_shapes=[
            vmem((toks, width), BF16),
            vmem((toks, width), BF16),
            vmem((toks, width), BF16),
            vmem((levels, heads, table), F32),
            vmem((levels, toks), jnp.int32),
            vmem((1, width), F32),
            vmem((toks, width), BF16),
            vmem((heads * DH, DH), BF16),
            vmem((shards, rows, DH), BF16),
            vmem((shards * (bits - 2), rows, DH), BF16),
            vmem((shards * (bits - 2), rows, DH), BF16),
            vmem((heads, DH, bits * DH), BF16),
            vmem((heads, DH, DH), BF16),
            vmem((levels, toks, width), F32),
            vmem((levels, toks, width), F32),
            vmem((2 * heads, CH, CH), F32),
            vmem((toks, width), BF16),
            vmem((2, toks), F32),
            vmem((members, 2, toks), F32),
            vmem((toks, width), BF16),
            vmem((1, width), F32),
            vmem((NX, 1, width), F32),
            vmem((1, width), F32),
            vmem((toks, width), BF16),
            vmem((shards * (bits - 2), rows, DH), BF16),
            vmem((shards * (bits - 2), rows, DH), BF16),
            vmem((heads, DH, DH), F32),
            vmem((shards, rows, DH), BF16),
            vmem((shards, rows, DH), BF16),
            vmem((toks, width), F32),
            vmem((toks, width), F32),
            vmem((levels, heads, table), F32),
            vmem((shards, heads, table), F32),
            vmem((toks, width), F32),
            vmem((toks, width), F32),
            vmem((2 * heads, CH, CH), BF16),
            vmem((heads, toks, bits * DH), BF16),
            vmem((NX, DH, DH), BF16),
            vmem((2 * NX, DH, DH), BF16),
            vmem((2 * NX, DH, DH), BF16),
            vmem((2 * NX, DH, DH), BF16),
            vmem((2 * NX, DH, DH), BF16),
            vmem((NX, DH, DH), BF16),
            vmem((NX, DH, DH), BF16),
            vmem((1, width), F32),
            vmem((shards // NX, 1, width), F32),
            vmem((heads, DH, toks), BF16),
            pltpu.SemaphoreType.DMA((7,)),
            pltpu.SemaphoreType.DMA((16,)),
            pltpu.SemaphoreType.DMA((16,)),
            pltpu.SemaphoreType.DMA((levels,)),
        ],
        compiler_params=pltpu.CompilerParams(
            collective_id=0, has_side_effects=True, vmem_limit_bytes=VMEM_BYTES
        ),
    )(
        *(
            pltpu.with_memory_space_constraint(array, pltpu.HBM)
            for array in (
                queries,
                key_rows,
                value_rows,
                jnp.transpose(level_table, (1, 2, 0)),
                jnp.transpose(level_index),
                norm_gain.reshape(1, features),
                cotangent,
            )
        )
    )
    normed, dq, dk, dv, gtab, ggain = pl.pallas_call(
        copy_kernel,
        out_shape=tuple(jax.ShapeDtypeStruct(o.shape, o.dtype) for o in outs),
        in_specs=[pl.BlockSpec(memory_space=pltpu.VMEM)] * 6,
        out_specs=[anywhere] * 6,
        scratch_shapes=[pltpu.SemaphoreType.DMA((6,))],
        compiler_params=pltpu.CompilerParams(vmem_limit_bytes=4 * 2**20),
    )(*outs)
    return normed, dq, dk, dv, jnp.transpose(gtab, (2, 0, 1)), ggain.reshape(features)


def solution(mesh):
    wide = P("seq", "head")
    rows = P(("seq", "head"), None)
    table = P(None, None, "head")
    return jax.shard_map(
        functools.partial(body, mesh.shape["seq"], mesh.shape["head"]),
        mesh=mesh,
        in_specs=(wide, wide, wide, table, P("seq", None), P(), rows),
        out_specs=(rows, wide, wide, wide, table, P()),
        check_vma=False,
    )
```
